256 devices in a mesh: seq: 32 (over z, y), head: 8 (over x, core).
Axes of the slice: x: 4, y: 4, z: 8, core: 2. Of those that a mesh axis runs over, the one named last changes fastest.
Arguments:
- queries: bfloat16 [4096, 24576], P('seq', 'head'), may hold values from -325 to 325
- latents: bfloat16 [4096, 576], P('seq'), may hold values from -5 to 5
- doc_ids: int32 [4096], P('seq'), may hold values from 0 to 15, never falling along the last dimension, each value on 1 to 512 neighbouring positions
- key_weight: bfloat16 [512, 16384], P(None, 'head'), may hold values from -0.25 to 0.25
- value_weight: bfloat16 [512, 16384], P(None, 'head'), may hold values from -0.25 to 0.25
- out_grad: bfloat16 [4096, 16384], P('seq', 'head'), may hold values from -6 to 6
Outputs:
- attended: bfloat16 [4096, 16384], P('seq', 'head')
- latent_grad: float32 [4096, 576], P('seq')
- key_weight_grad: float32 [512, 16384], P('seq', 'head')
- value_weight_grad: float32 [512, 16384], P('seq', 'head')
The draws below stay inside these ranges and needn't reach their ends.
Inputs may be any that keep to these rules, and one draw needn't show every extreme that they name: `doc_ids`: ids never fall along the sequence; every document holds 1 to 512 tokens, and one holds exactly that many.
All inputs are finite; a program needn't handle non-finite values.
Results may differ from the reference program's by a relative error of at most 0.028.
Values may be sent and summed in bfloat16 or wider, within the bound.
No kernel may reach another device: no remote copies, remote signals or barrier semaphores. Data moves between devices by JAX's collectives and lax.ppermute only.
A program may use at most 128 MiB of HBM per device.

```python
import math
import jax
import jax.numpy as jnp
import numpy as np
from jax import lax

HEADS = 128
NOPE = 128
ROPE = 64
VDIM = 128
LATENT = 512
TOK_DEV = 128
REACH = 4
TOKENS = 4096
DOCS = 16


def base_latents(key):
    normal_rows = jax.random.normal(jax.random.fold_in(key, 7), (TOKENS, LATENT + ROPE), jnp.float32)
    return jnp.clip(normal_rows, -5.0, 5.0)


def draw_latents(key, part):
    drawn = base_latents(key)
    return drawn.astype(jnp.bfloat16)


def draw_queries(key, part):
    width = NOPE + ROPE
    drawn = jax.random.normal(jax.random.fold_in(key, 3), (TOKENS, HEADS, width), jnp.float32)
    drawn = jnp.clip(drawn, -5.0, 5.0)
    return drawn.reshape(TOKENS, HEADS * width).astype(jnp.bfloat16)


def shard_levels(stream_key, dims, shards, low, high):
    level = 1.0
    for dim, parts in shards:
        steps = jax.random.uniform(jax.random.fold_in(jax.random.fold_in(stream_key, 6), dim), (parts,), jnp.float32, low / len(shards), high / len(shards))
        level = level * jnp.repeat(jnp.exp(steps), dims[dim] // parts).reshape((-1,) + (1,) * (len(dims) - 1 - dim))
    return level


def split_up(count, total, limit, lean):
    weights = [(1 << 20) // math.isqrt(standing ** lean) + 1 for standing in range(2, count + 1)]
    rest, given = total - limit - (count - 1), [1] * (count - 1)
    while rest > 0:
        movable = [i for i in range(count - 1) if given[i] < limit]
        pool, budget = sum([weights[i] for i in movable]), rest
        for i in movable:
            more = min(limit - given[i], max(1, budget * weights[i] // pool), rest)
            given[i] = given[i] + more
            rest = rest - more
    return np.array([limit] + given)


def ragged_sizes(own_key, number_of, total, reach, lean):
    if number_of == 2:
        one = jax.random.randint(own_key, (), max(1, total - reach), min(reach, total - 1) + 1)
        return jnp.stack([one, total - one])
    sizes = jnp.asarray(split_up(number_of, total, reach, lean), jnp.int32)
    pairs = (number_of - 1) // 2
    giver, taker = sizes[1:1 + 2 * pairs:2], sizes[2:2 + 2 * pairs:2]
    room = jnp.minimum(giver - 1, reach - taker)
    passed = jax.random.randint(jax.random.fold_in(own_key, 1), (pairs,), 0, 1 << 20) % (room + 1)
    sizes = sizes.at[1:1 + 2 * pairs:2].set(giver - passed).at[2:2 + 2 * pairs:2].set(taker + passed)
    return sizes[jax.random.permutation(jax.random.fold_in(own_key, 2), number_of)]


def normal_values(own_key, extent, deviation, bound, split=(), held_as=jnp.bfloat16):
    factor_of = shard_levels(own_key, extent, split, -0.22, 0.18) if split else 1.0
    values = jax.random.normal(own_key, extent, jnp.float32) * deviation * factor_of
    return jnp.minimum(jnp.maximum(values, -bound), bound).astype(held_as)


def setup_inputs(seed: int = 0) -> dict:
    seeds = jax.random.split(jax.random.key(seed), 7)
    queries = draw_queries(jax.random.fold_in(seeds[6], 71), 0)
    latents = draw_latents(jax.random.fold_in(seeds[6], 71), 0)
    doc_ids = jnp.searchsorted(jnp.cumsum(ragged_sizes(seeds[2], DOCS, TOKENS, REACH * TOK_DEV, 1)), jnp.arange(TOKENS), side="right").astype(jnp.int32)
    key_weight = normal_values(seeds[3], (LATENT, HEADS * NOPE), LATENT ** -0.5, 0.25, ((1, 8),))
    value_weight = normal_values(seeds[4], (LATENT, HEADS * VDIM), LATENT ** -0.5, 0.25, ((1, 8),))
    out_grad = normal_values(seeds[5], (TOKENS, HEADS * VDIM), 1.0, 6.0, ((0, 32), (1, 8)))
    return {"queries": queries, "latents": latents, "doc_ids": doc_ids, "key_weight": key_weight, "value_weight": value_weight, "out_grad": out_grad}


def reference(queries, latents, doc_ids, key_weight, value_weight, out_grad):
    query_width = NOPE + ROPE
    score_scale = 1.0 / (query_width ** 0.5)
    block_count = TOKENS // TOK_DEV
    key_rows = (REACH + 1) * TOK_DEV
    lead_rows = REACH * TOK_DEV
    latent_part = latents[:, :LATENT]
    k_nope = jnp.dot(latent_part, key_weight, preferred_element_type=jnp.float32).astype(jnp.bfloat16)
    values_up = jnp.dot(latent_part, value_weight, preferred_element_type=jnp.float32).astype(jnp.bfloat16)
    nope_pad = jnp.concatenate([jnp.zeros((lead_rows, HEADS * NOPE), jnp.bfloat16), k_nope], axis=0)
    value_pad = jnp.concatenate([jnp.zeros((lead_rows, HEADS * VDIM), jnp.bfloat16), values_up], axis=0)
    rope_pad = jnp.concatenate([jnp.zeros((lead_rows, ROPE), jnp.bfloat16), latents[:, LATENT:]], axis=0)
    latent_pad = jnp.concatenate([jnp.zeros((lead_rows, LATENT), jnp.bfloat16), latent_part], axis=0)
    ids_pad = jnp.concatenate([jnp.full((lead_rows,), -1, jnp.int32), doc_ids.astype(jnp.int32)], axis=0)
    pos_pad = jnp.arange(TOKENS + lead_rows, dtype=jnp.int32) - lead_rows

    def block_step(totals, block_index):
        first_row = (block_index * TOK_DEV).astype(jnp.int32)
        query_heads = lax.dynamic_slice_in_dim(queries, first_row, TOK_DEV, 0).reshape(TOK_DEV, HEADS, query_width).astype(jnp.float32)
        grad_heads = lax.dynamic_slice_in_dim(out_grad, first_row, TOK_DEV, 0).reshape(TOK_DEV, HEADS, VDIM).astype(jnp.float32)
        query_ids = lax.dynamic_slice_in_dim(doc_ids.astype(jnp.int32), first_row, TOK_DEV, 0)
        query_pos = first_row + jnp.arange(TOK_DEV, dtype=jnp.int32)
        key_heads = lax.dynamic_slice_in_dim(nope_pad, first_row, key_rows, 0)
        value_heads = lax.dynamic_slice_in_dim(value_pad, first_row, key_rows, 0)
        key_rope = lax.dynamic_slice_in_dim(rope_pad, first_row, key_rows, 0).astype(jnp.float32)
        latent_rows = lax.dynamic_slice_in_dim(latent_pad, first_row, key_rows, 0)
        key_ids = lax.dynamic_slice_in_dim(ids_pad, first_row, key_rows, 0)
        key_pos = lax.dynamic_slice_in_dim(pos_pad, first_row, key_rows, 0)
        key_f = key_heads.reshape(key_rows, HEADS, NOPE).astype(jnp.float32)
        value_f = value_heads.reshape(key_rows, HEADS, VDIM).astype(jnp.float32)
        scores = jnp.einsum("phd,thd->hpt", query_heads[:, :, :NOPE], key_f, precision=lax.Precision.HIGHEST)
        scores = scores + jnp.einsum("phr,tr->hpt", query_heads[:, :, NOPE:], key_rope, precision=lax.Precision.HIGHEST)
        scores = scores * score_scale
        visible = (key_pos[None, :] <= query_pos[:, None]) & (key_ids[None, :] == query_ids[:, None])
        scores = jnp.where(visible[None], scores, -jnp.inf)
        row_top = jnp.max(scores, axis=-1, keepdims=True)
        row_lse = row_top + jnp.log(jnp.sum(jnp.exp(scores - row_top), axis=-1, keepdims=True))
        weight_f = jnp.exp(scores - row_lse)
        weight_b = weight_f.astype(jnp.bfloat16)
        output = jnp.einsum("hpt,thd->phd", weight_b.astype(jnp.float32), value_f, precision=lax.Precision.HIGHEST).astype(jnp.bfloat16)
        d_weight = jnp.einsum("phd,thd->hpt", grad_heads, value_f, precision=lax.Precision.HIGHEST)
        row_delta = jnp.sum(grad_heads * output.astype(jnp.float32), axis=-1)
        d_score = (weight_f * (d_weight - jnp.transpose(row_delta)[:, :, None]) * score_scale).astype(jnp.bfloat16)
        d_key = jnp.einsum("hpt,phd->thd", d_score.astype(jnp.float32), query_heads, precision=lax.Precision.HIGHEST).astype(jnp.bfloat16)
        d_value = jnp.einsum("hpt,phd->thd", weight_b.astype(jnp.float32), grad_heads, precision=lax.Precision.HIGHEST).astype(jnp.bfloat16)
        key_nope_grad = d_key[:, :, :NOPE].reshape(key_rows, HEADS * NOPE)
        value_grad = d_value.reshape(key_rows, HEADS * VDIM)
        latent_term = jnp.dot(key_nope_grad, jnp.transpose(key_weight), preferred_element_type=jnp.float32)
        latent_term = latent_term + jnp.dot(value_grad, jnp.transpose(value_weight), preferred_element_type=jnp.float32)
        rope_term = jnp.sum(d_key[:, :, NOPE:].astype(jnp.float32), axis=1)
        partial_grad = jnp.concatenate([latent_term, rope_term], axis=1)
        key_total = totals[0] + jnp.dot(jnp.transpose(latent_rows), key_nope_grad, preferred_element_type=jnp.float32)
        value_total = totals[1] + jnp.dot(jnp.transpose(latent_rows), value_grad, preferred_element_type=jnp.float32)
        return (key_total, value_total), (output.reshape(TOK_DEV, HEADS * VDIM), partial_grad)

    start_totals = (jnp.zeros((LATENT, HEADS * NOPE), jnp.float32), jnp.zeros((LATENT, HEADS * VDIM), jnp.float32))
    totals, emitted = lax.scan(block_step, start_totals, jnp.arange(block_count, dtype=jnp.int32))
    attended = emitted[0].reshape(TOKENS, HEADS * VDIM)
    pieces = emitted[1].reshape(block_count, REACH + 1, TOK_DEV, LATENT + ROPE)
    summed = jnp.zeros((block_count + REACH, TOK_DEV, LATENT + ROPE), jnp.float32)
    for offset in range(REACH + 1):
        summed = summed + jnp.pad(pieces[:, offset], ((offset, REACH - offset), (0, 0), (0, 0)))
    latent_grad = summed[REACH:].reshape(TOKENS, LATENT + ROPE)
    return attended, latent_grad, totals[0], totals[1]
```

```python
import functools
import math

import jax
import jax.numpy as jnp
from jax import lax
from jax.experimental import pallas as pl
from jax.experimental.pallas import tpu as pltpu
from jax.sharding import Mesh
from jax.sharding import PartitionSpec as P

NOPE = 128
ROPE = 64
VDIM = 128
LATENT = 512
TOK = 128
ROWS = 4 * TOK
KEYS = 2 * ROWS
TILE = 256
SPAN = ROWS + TILE
PAY = 640
SCALE = 1.0 / math.sqrt(NOPE + ROPE)
LOG2E = math.log2(math.e)
HIDDEN = -1e30
GROUPS = 8
F32 = jnp.float32
BF16 = jnp.bfloat16


def nt(a, b):
    return lax.dot_general(a, b, (((1,), (1,)), ((), ())), preferred_element_type=F32)


def nn(a, b):
    return lax.dot_general(a, b, (((1,), (0,)), ((), ())), preferred_element_type=F32)


def tn(a, b):
    return lax.dot_general(a, b, (((0,), (0,)), ((), ())), preferred_element_type=F32)


def pair_kernel(first, where_ref, x_ref, l_ref, wk_ref, wv_ref, *refs):
    if first:
        out_ref, dw_ref, dl_ref, kcat, vals, bias, dk_acc, dv_acc, grads = refs
        before_ref = None
    else:
        before_ref, out_ref, dw_ref, dl_ref, kcat, vals, bias, dk_acc, dv_acc, grads = refs
    group = where_ref[0]
    lat = l_ref[:, :LATENT]
    tail = l_ref[:, LATENT:].astype(F32)
    lane = lax.broadcasted_iota(jnp.int32, (KEYS, 128), 1)
    low = lane < ROPE

    key_id = tail[:, ROPE : ROPE + 1]
    key_row = lax.broadcasted_iota(jnp.int32, (KEYS, 1), 0)
    key_id = jnp.where((key_row < ROWS) & (group == 0), -1.0, key_id)
    query_id = jnp.transpose(tail[ROWS:])[ROPE : ROPE + 1, :]
    for i in range(2):
        start = i * TILE
        at = lax.broadcasted_iota(jnp.int32, (SPAN, TILE), 0)
        by = lax.broadcasted_iota(jnp.int32, (SPAN, TILE), 1)
        seen = (key_id[start : start + SPAN] == query_id[:, start : start + TILE]) & (
            at <= by + ROWS
        )
        bias[i] = jnp.where(seen, 0.0, HIDDEN)

    keys_up = nn(lat, wk_ref[...])
    vals_up = nn(lat, wv_ref[...])
    vals[...] = vals_up.astype(BF16)
    rope_low = jnp.where(low, tail, 0.0)
    rope_high = pltpu.roll(rope_low, ROPE, 1)
    turned = pltpu.roll(keys_up[:, NOPE:], ROPE, 1)
    kcat[0, :, :NOPE] = keys_up[:, :NOPE].astype(BF16)
    kcat[0, :, NOPE:] = rope_low.astype(BF16)
    kcat[1, :, :NOPE] = jnp.where(low, 0.0, turned).astype(BF16)
    kcat[1, :, NOPE:] = jnp.where(low, turned, rope_high).astype(BF16)

    for h in range(2):
        v_turned = jnp.transpose(vals_up[:, h * VDIM : (h + 1) * VDIM]).astype(BF16)
        for i in range(2):
            start = i * TILE
            span = slice(start, start + SPAN)
            rows = slice(start, start + TILE)
            qc = x_ref[rows, h * NOPE : h * NOPE + 256]
            og = x_ref[rows, 384 + h * VDIM : 384 + (h + 1) * VDIM]
            s = nt(kcat[h, span, :], qc) * (SCALE * LOG2E) + bias[i]
            top = jnp.max(s, axis=0, keepdims=True)
            e = jnp.exp2(s - top)
            p = e * (1.0 / jnp.sum(e, axis=0, keepdims=True))
            pb = p.astype(BF16)
            out_t = nn(v_turned[:, span], pb).astype(BF16).astype(F32)
            out_ref[rows, h * VDIM : (h + 1) * VDIM] = jnp.transpose(out_t).astype(BF16)
            og_t = jnp.transpose(og.astype(F32))
            delta = jnp.sum(og_t * out_t, axis=0, keepdims=True)
            dp = nn(vals[span, h * VDIM : (h + 1) * VDIM], og_t.astype(BF16))
            ds = (p * (dp - delta) * SCALE).astype(BF16)
            dk = nn(ds, qc)
            dv = nn(pb, og)
            if i == 0:
                dk_acc[h, :SPAN, :] = dk
                dv_acc[:SPAN, :] = dv
            else:
                dk_acc[h, TILE:ROWS + TILE, :] += dk[:ROWS]
                dv_acc[TILE:ROWS + TILE, :] += dv[:ROWS]
                dk_acc[h, SPAN:, :] = dk[ROWS:]
                dv_acc[SPAN:, :] = dv[ROWS:]
        grads[:, 256 + h * VDIM : 256 + (h + 1) * VDIM] = dv_acc[...].astype(BF16)
    grads[:, :NOPE] = dk_acc[0, :, :NOPE].astype(BF16)
    mixed = jnp.where(low, dk_acc[1, :, NOPE:], dk_acc[1, :, :NOPE])
    grads[:, NOPE : 2 * NOPE] = pltpu.roll(mixed, ROPE, 1).astype(BF16)
    rope_grad = jnp.where(low, dk_acc[0, :, NOPE:], dk_acc[1, :, NOPE:])
    rope_grad = rope_grad + pltpu.roll(rope_grad, ROPE, 1)
    dl = nt(grads[:, :256], wk_ref[...]) + nt(grads[:, 256:], wv_ref[...])
    if not first:
        dl = dl + before_ref[:, :LATENT]
        rope_grad = rope_grad + before_ref[:, LATENT:]
    dl_ref[:, :LATENT] = dl.astype(dl_ref.dtype)
    dl_ref[:, LATENT:] = rope_grad.astype(dl_ref.dtype)
    dw_ref[...] = tn(lat, grads[...]).astype(BF16)


def pair_call(pair, place, x, lat, key_weight, value_weight, before):
    first = before is None

    def whole(*shape):
        return pl.BlockSpec(shape, lambda i, w: (0,) * len(shape))

    weight_spec = pl.BlockSpec((LATENT, 256), lambda i, w: (0, 2 * w[1] + pair))
    in_specs = [whole(ROWS, PAY), whole(KEYS, PAY), weight_spec, weight_spec]
    args = [x, lat, key_weight, value_weight]
    if not first:
        in_specs.append(whole(KEYS, PAY))
        args.append(before)
    return pl.pallas_call(
        functools.partial(pair_kernel, first),
        grid_spec=pltpu.PrefetchScalarGridSpec(
            num_scalar_prefetch=1,
            grid=(1,),
            in_specs=in_specs,
            out_specs=[whole(ROWS, 256), whole(LATENT, 512), whole(KEYS, PAY)],
            scratch_shapes=[
                pltpu.VMEM((2, KEYS, 256), BF16),
                pltpu.VMEM((KEYS, 256), BF16),
                pltpu.VMEM((2, SPAN, TILE), F32),
                pltpu.VMEM((2, KEYS, 256), F32),
                pltpu.VMEM((KEYS, VDIM), F32),
                pltpu.VMEM((KEYS, 512), BF16),
            ],
        ),
        out_shape=[
            jax.ShapeDtypeStruct((ROWS, 256), BF16),
            jax.ShapeDtypeStruct((LATENT, 512), BF16),
            jax.ShapeDtypeStruct((KEYS, PAY), F32 if first else BF16),
        ],
        compiler_params=pltpu.CompilerParams(vmem_limit_bytes=48 << 20),
        cost_estimate=pl.CostEstimate(
            flops=4_000_000_000, bytes_accessed=8_000_000, transcendentals=800_000
        ),
        name="pair",
    )(place, *args)


def exchanged(x, axes):
    return lax.all_to_all(x, axes, split_axis=0, concat_axis=0, tiled=True)


def sent_to_all(x, axes):
    copies = jnp.broadcast_to(x, (lax.axis_size(axes), *x.shape))
    return exchanged(copies, axes)


def per_device(queries, latents, doc_ids, key_weight, value_weight, out_grad):
    group = lax.axis_index("z")
    place = jnp.stack([group, lax.axis_index("y")]).astype(jnp.int32)
    pay = jnp.concatenate(
        [latents, doc_ids.astype(BF16)[:, None], jnp.zeros((TOK, PAY - 577), BF16)], axis=1
    )
    ahead = [(i, i + 1) for i in range(GROUPS - 1)]
    behind = [(i + 1, i) for i in range(GROUPS - 1)]
    q_parts = queries.reshape(TOK, 4, 2, 384)
    g_parts = out_grad.reshape(TOK, 4, 2, 256)
    earlier = lax.ppermute(pay, "z", ahead)
    xs = []
    for pair in range(2):
        x = jnp.concatenate([q_parts[:, :, pair], g_parts[:, :, pair]], axis=-1)
        xs.append(exchanged(jnp.transpose(x, (1, 0, 2)), "y").reshape(ROWS, PAY))
    lat = sent_to_all(jnp.stack([earlier, pay]), "y")
    lat = jnp.transpose(lat, (1, 0, 2, 3)).reshape(KEYS, PAY)

    out0, dw0, dl = pair_call(0, place, xs[0], lat, key_weight, value_weight, None)
    out0 = exchanged(out0.reshape(4, TOK, 256), "y")
    dw0 = exchanged(dw0.reshape(32, 16, 512), ("z", "y"))
    out1, dw1, dl = pair_call(1, place, xs[1], lat, key_weight, value_weight, dl)
    dl = dl.reshape(2, 4, 8, 16, PAY).transpose(1, 2, 0, 3, 4).reshape(32, 32, PAY)
    dl = exchanged(dl, ("y", "x", "core")).astype(F32).sum(axis=0)
    dw1 = exchanged(dw1.reshape(32, 16, 512), ("z", "y"))
    out1 = exchanged(out1.reshape(4, TOK, 256), "y")
    own = dl[16:] + lax.ppermute(dl[:16].astype(BF16), "z", behind).astype(F32)
    latent_grad = sent_to_all(own.astype(BF16), ("x", "core")).astype(F32)
    latent_grad = latent_grad.reshape(TOK, PAY)[:, : LATENT + ROPE]
    attended = jnp.stack([out0, out1], axis=1).transpose(2, 0, 1, 3).reshape(TOK, 2048)
    dw = jnp.stack([dw0, dw1], axis=1).reshape(GROUPS, 4, 2, 16, 512).astype(F32).sum(axis=0)
    dw = dw.transpose(2, 0, 1, 3)
    key_grad = dw[..., :256].reshape(16, 2048)
    value_grad = dw[..., 256:].reshape(16, 2048)
    return attended, latent_grad, key_grad, value_grad


def solution(mesh):
    split = Mesh(mesh.devices.reshape(GROUPS, 4, 4, 2), ("z", "y", "x", "core"))
    seq, head = ("z", "y"), ("x", "core")
    in_specs = (P(seq, head), P(seq, None), P(seq), P(None, head), P(None, head), P(seq, head))
    out_specs = (P(seq, head), P(seq, None), P(seq, head), P(seq, head))
    return jax.shard_map(
        per_device, mesh=split, in_specs=in_specs, out_specs=out_specs, check_vma=False
    )
```

```python
import functools
import math

import jax
import jax.numpy as jnp
from jax import lax
from jax.experimental import pallas as pl
from jax.experimental.pallas import tpu as pltpu
from jax.sharding import Mesh
from jax.sharding import PartitionSpec as P

NOPE = 128
ROPE = 64
VDIM = 128
LATENT = 512
TOK = 128
ROWS = 4 * TOK
KEYS = 2 * ROWS
TILE = 256
SPAN = ROWS + TILE
PAY = 640
SCALE = 1.0 / math.sqrt(NOPE + ROPE)
LOG2E = math.log2(math.e)
HIDDEN = -1e30
GROUPS = 8
F32 = jnp.float32
BF16 = jnp.bfloat16


def nt(a, b):
    return lax.dot_general(a, b, (((1,), (1,)), ((), ())), preferred_element_type=F32)


def nn(a, b):
    return lax.dot_general(a, b, (((1,), (0,)), ((), ())), preferred_element_type=F32)


def tn(a, b):
    return lax.dot_general(a, b, (((0,), (0,)), ((), ())), preferred_element_type=F32)


def pack_kernel(where_ref, q_ref, g_ref, *piece_refs):
    y = where_ref[1]
    for k in range(4):
        to = (y + k) & 3
        for pair in range(2):
            piece = piece_refs[4 * pair + k]
            piece[:, :384] = q_ref[:, pl.ds(pl.multiple_of(to * 768 + pair * 384, 128), 384)]
            piece[:, 384:] = g_ref[:, pl.ds(pl.multiple_of(to * 512 + pair * 256, 128), 256)]


def pack_call(place, queries, out_grad):
    vmem = pl.BlockSpec(memory_space=pltpu.VMEM)
    return pl.pallas_call(
        pack_kernel,
        in_specs=[pl.BlockSpec(memory_space=pltpu.SMEM), vmem, vmem],
        out_specs=[vmem] * 8,
        out_shape=[jax.ShapeDtypeStruct((TOK, PAY), BF16)] * 8,
        cost_estimate=pl.CostEstimate(flops=0, bytes_accessed=2_600_000, transcendentals=0),
        name="pack",
    )(place, queries, out_grad)


def pair_kernel(first, where_ref, *refs):
    pieces, refs = refs[:4], refs[4:]
    mine_ref, other_ref, wk_ref, wv_ref, refs = *refs[:4], refs[4:]
    if first:
        before_ref, refs = None, refs
        (dl_ref,), outs = refs[:1], refs[1:]
    else:
        before_ref, refs = refs[0], refs[1:]
        keep_ref, send_ref, outs = refs[0], refs[1], refs[2:]
    out_refs, dw_ref = outs[:4], outs[4]
    x_ref, l_ref, kcat, vals, bias, dk_acc, dv_acc, grads, attended, dl_acc = outs[5:]
    group, y, core = where_ref[0], where_ref[1], where_ref[2]
    half = TOK // 2
    for k in range(4):
        block = (y - k) & 3
        x_ref[pl.ds(pl.multiple_of(block * TOK, TOK), TOK), :] = pieces[k][...]
        for back in range(2):
            row = (1 - back) * ROWS + block * TOK
            own = pl.multiple_of(row + core * half, half)
            l_ref[pl.ds(own, half), :] = mine_ref[4 * back + k]
            swapped = pl.multiple_of(row + (1 - core) * half, half)
            l_ref[pl.ds(swapped, half), :] = other_ref[4 * back + k]
    lat = l_ref[:, :LATENT]
    tail = l_ref[:, LATENT:].astype(F32)
    lane = lax.broadcasted_iota(jnp.int32, (KEYS, 128), 1)
    low = lane < ROPE

    key_id = tail[:, ROPE : ROPE + 1]
    key_row = lax.broadcasted_iota(jnp.int32, (KEYS, 1), 0)
    key_id = jnp.where((key_row < ROWS) & (group == 0), -1.0, key_id)
    query_id = jnp.transpose(tail[ROWS:])[ROPE : ROPE + 1, :]
    for i in range(2):
        start = i * TILE
        at = lax.broadcasted_iota(jnp.int32, (SPAN, TILE), 0)
        by = lax.broadcasted_iota(jnp.int32, (SPAN, TILE), 1)
        seen = (key_id[start : start + SPAN] == query_id[:, start : start + TILE]) & (
            at <= by + ROWS
        )
        bias[i] = jnp.where(seen, 0.0, HIDDEN)

    keys_up = nn(lat, wk_ref[...])
    vals_up = nn(lat, wv_ref[...])
    vals[...] = vals_up.astype(BF16)
    rope_low = jnp.where(low, tail, 0.0)
    rope_high = pltpu.roll(rope_low, ROPE, 1)
    turned = pltpu.roll(keys_up[:, NOPE:], ROPE, 1)
    kcat[0, :, :NOPE] = keys_up[:, :NOPE].astype(BF16)
    kcat[0, :, NOPE:] = rope_low.astype(BF16)
    kcat[1, :, :NOPE] = jnp.where(low, 0.0, turned).astype(BF16)
    kcat[1, :, NOPE:] = jnp.where(low, turned, rope_high).astype(BF16)

    for h in range(2):
        v_turned = jnp.transpose(vals_up[:, h * VDIM : (h + 1) * VDIM]).astype(BF16)
        for i in range(2):
            start = i * TILE
            span = slice(start, start + SPAN)
            rows = slice(start, start + TILE)
            qc = x_ref[rows, h * NOPE : h * NOPE + 256]
            og = x_ref[rows, 384 + h * VDIM : 384 + (h + 1) * VDIM]
            s = nt(kcat[h, span, :], qc) * (SCALE * LOG2E) + bias[i]
            top = jnp.max(s, axis=0, keepdims=True)
            e = jnp.exp2(s - top)
            p = e * (1.0 / jnp.sum(e, axis=0, keepdims=True))
            pb = p.astype(BF16)
            out_t = nn(v_turned[:, span], pb).astype(BF16).astype(F32)
            attended[rows, h * VDIM : (h + 1) * VDIM] = jnp.transpose(out_t).astype(BF16)
            og_t = jnp.transpose(og.astype(F32))
            delta = jnp.sum(og_t * out_t, axis=0, keepdims=True)
            dp = nn(vals[span, h * VDIM : (h + 1) * VDIM], og_t.astype(BF16))
            ds = (p * (dp - delta) * SCALE).astype(BF16)
            dk = nn(ds, qc)
            dv = nn(pb, og)
            if i == 0:
                dk_acc[h, :SPAN, :] = dk
                dv_acc[:SPAN, :] = dv
            else:
                dk_acc[h, TILE : ROWS + TILE, :] += dk[:ROWS]
                dv_acc[TILE : ROWS + TILE, :] += dv[:ROWS]
                dk_acc[h, SPAN:, :] = dk[ROWS:]
                dv_acc[SPAN:, :] = dv[ROWS:]
        grads[:, 256 + h * VDIM : 256 + (h + 1) * VDIM] = dv_acc[...].astype(BF16)
    for k in range(4):
        to = pl.multiple_of(((y + k) & 3) * TOK, TOK)
        out_refs[k][...] = attended[pl.ds(to, TOK), :]
    grads[:, :NOPE] = dk_acc[0, :, :NOPE].astype(BF16)
    mixed = jnp.where(low, dk_acc[1, :, NOPE:], dk_acc[1, :, :NOPE])
    grads[:, NOPE : 2 * NOPE] = pltpu.roll(mixed, ROPE, 1).astype(BF16)
    rope_grad = jnp.where(low, dk_acc[0, :, NOPE:], dk_acc[1, :, NOPE:])
    rope_grad = rope_grad + pltpu.roll(rope_grad, ROPE, 1)
    dl = nt(grads[:, :256], wk_ref[...]) + nt(grads[:, 256:], wv_ref[...])
    if first:
        dl_ref[:, :LATENT] = dl
        dl_ref[:, LATENT:] = rope_grad
    else:
        dl_acc[:, :LATENT] = (dl + before_ref[:, :LATENT]).astype(BF16)
        dl_acc[:, LATENT:] = (rope_grad + before_ref[:, LATENT:]).astype(BF16)
        for k in range(4):
            for back in range(2):
                row = (1 - back) * ROWS + ((y + k) & 3) * TOK
                own = pl.multiple_of(row + core * half, half)
                keep_ref[k, back * half : (back + 1) * half, :] = dl_acc[pl.ds(own, half), :]
                swapped = pl.multiple_of(row + (1 - core) * half, half)
                send_ref[k, back * half : (back + 1) * half, :] = dl_acc[pl.ds(swapped, half), :]
    dw_ref[...] = tn(lat, grads[...]).astype(BF16)


def pair_call(pair, place, pieces, mine, other, key_weight, value_weight, before):
    first = before is None

    def whole(*shape):
        return pl.BlockSpec(shape, lambda i, w: (0,) * len(shape))

    weight_spec = pl.BlockSpec((LATENT, 256), lambda i, w: (0, 2 * w[1] + pair))
    in_specs = [whole(TOK, PAY)] * 4 + [whole(8, TOK // 2, PAY)] * 2 + [weight_spec] * 2
    args = [*pieces, mine, other, key_weight, value_weight]
    if first:
        dl_shapes = [jax.ShapeDtypeStruct((KEYS, PAY), F32)]
    else:
        in_specs.append(whole(KEYS, PAY))
        args.append(before)
        dl_shapes = [jax.ShapeDtypeStruct((4, TOK, PAY), BF16)] * 2
    out_shape = dl_shapes + [jax.ShapeDtypeStruct((TOK, 256), BF16)] * 4
    out_shape.append(jax.ShapeDtypeStruct((LATENT, 512), BF16))
    return pl.pallas_call(
        functools.partial(pair_kernel, first),
        grid_spec=pltpu.PrefetchScalarGridSpec(
            num_scalar_prefetch=1,
            grid=(1,),
            in_specs=in_specs,
            out_specs=[whole(*leaf.shape) for leaf in out_shape],
            scratch_shapes=[
                pltpu.VMEM((ROWS, PAY), BF16),
                pltpu.VMEM((KEYS, PAY), BF16),
                pltpu.VMEM((2, KEYS, 256), BF16),
                pltpu.VMEM((KEYS, 256), BF16),
                pltpu.VMEM((2, SPAN, TILE), F32),
                pltpu.VMEM((2, KEYS, 256), F32),
                pltpu.VMEM((KEYS, VDIM), F32),
                pltpu.VMEM((KEYS, 512), BF16),
                pltpu.VMEM((ROWS, 256), BF16),
                pltpu.VMEM((KEYS, PAY), BF16),
            ],
        ),
        out_shape=out_shape,
        compiler_params=pltpu.CompilerParams(vmem_limit_bytes=48 << 20),
        cost_estimate=pl.CostEstimate(
            flops=4_000_000_000, bytes_accessed=8_000_000, transcendentals=800_000
        ),
        name="pair",
    )(place, *args)


def latent_kernel(where_ref, *refs):
    terms, out_ref, held = refs[:8], refs[8], refs[9]
    x = where_ref[3]
    for k in range(4):
        held[(x - k) & 3] = terms[k][...].astype(F32)
        held[4 + ((x - k) & 3)] = terms[4 + k][...].astype(F32)
    total = held[0]
    for k in range(1, 8):
        total = total + held[k]
    out_ref[...] = total


def latent_call(place, terms):
    vmem = pl.BlockSpec(memory_space=pltpu.VMEM)
    return pl.pallas_call(
        latent_kernel,
        in_specs=[pl.BlockSpec(memory_space=pltpu.SMEM)] + [vmem] * 8,
        out_specs=vmem,
        out_shape=jax.ShapeDtypeStruct((TOK // 2, PAY), F32),
        scratch_shapes=[pltpu.VMEM((8, TOK // 2, PAY), F32)],
        name="latent",
    )(place, *terms)


def attended_kernel(where_ref, *refs):
    pieces, out_ref = refs[:8], refs[8]
    y = where_ref[1]
    for pair in range(2):
        for k in range(4):
            column = pl.multiple_of(((y - k) & 3) * 512 + pair * 256, 128)
            out_ref[:, pl.ds(column, 256)] = pieces[4 * pair + k][...]


def attended_call(place, pieces):
    vmem = pl.BlockSpec(memory_space=pltpu.VMEM)
    return pl.pallas_call(
        attended_kernel,
        in_specs=[pl.BlockSpec(memory_space=pltpu.SMEM)] + [vmem] * 8,
        out_specs=vmem,
        out_shape=jax.ShapeDtypeStruct((TOK, 2048), BF16),
        name="attended",
    )(place, *pieces)


def weight_kernel(first_ref, second_ref, key_ref, value_ref):
    for pair, ref in enumerate((first_ref, second_ref)):
        for y in range(4):
            total = ref[y].astype(F32)
            for z in range(1, GROUPS):
                total = total + ref[4 * z + y].astype(F32)
            column = y * 512 + pair * 256
            key_ref[:, column : column + 256] = total[:, :256]
            value_ref[:, column : column + 256] = total[:, 256:]


def weight_call(first, second):
    vmem = pl.BlockSpec(memory_space=pltpu.VMEM)
    return pl.pallas_call(
        weight_kernel,
        in_specs=[vmem] * 2,
        out_specs=[vmem] * 2,
        out_shape=[jax.ShapeDtypeStruct((16, 2048), F32)] * 2,
        name="weight",
    )(first, second)


def exchanged(x, axes):
    return lax.all_to_all(x, axes, split_axis=0, concat_axis=0, tiled=True)


def moved(value, ahead, along, size, step):
    if not ahead:
        return lax.ppermute(value, along, [(i, (i + step) % size) for i in range(size)])
    pairs = []
    for group in range(GROUPS):
        if 0 <= group + ahead < GROUPS:
            for i in range(size):
                pairs.append((group * size + i, (group + ahead) * size + (i + step) % size))
    return lax.ppermute(value, ("z", along), pairs)


def swapped(value):
    return lax.ppermute(value, "core", [(0, 1), (1, 0)])


def per_device(queries, latents, doc_ids, key_weight, value_weight, out_grad):
    core = lax.axis_index("core")
    place = [lax.axis_index("z"), lax.axis_index("y"), core, lax.axis_index("x")]
    place = jnp.stack(place).astype(jnp.int32)
    half = TOK // 2
    rows = lax.dynamic_slice_in_dim(latents, core * half, half)
    ids = lax.dynamic_slice_in_dim(doc_ids, core * half, half)
    pay = jnp.concatenate(
        [rows, ids.astype(BF16)[:, None], jnp.zeros((half, PAY - 577), BF16)], axis=1
    )
    mine = [pay] + [moved(pay, 0, "y", 4, k) for k in range(1, 4)]
    mine = jnp.stack(mine + [moved(pay, 1, "y", 4, k) for k in range(4)])
    other = swapped(mine)
    pieces = pack_call(place, queries, out_grad)
    pieces = [p if i % 4 == 0 else moved(p, 0, "y", 4, i % 4) for i, p in enumerate(pieces)]

    dl, *outs, dw0 = pair_call(
        0, place, pieces[:4], mine, other, key_weight, value_weight, None
    )
    dw0 = exchanged(dw0.reshape(32, 16, 512), ("z", "y"))
    keep, send, *outs1, dw1 = pair_call(
        1, place, pieces[4:], mine, other, key_weight, value_weight, dl
    )
    dw1 = exchanged(dw1.reshape(32, 16, 512), ("z", "y"))
    outs = [p if i % 4 == 0 else moved(p, 0, "y", 4, i % 4) for i, p in enumerate(outs + outs1)]
    attended = attended_call(place, outs)

    came = swapped(send)
    both = [(keep[k].astype(F32) + came[k].astype(F32)) for k in range(4)]
    total = both[0]
    for k in range(1, 4):
        total = total + moved(both[k].astype(BF16), 0, "y", 4, k).astype(F32)
    total = total.astype(BF16)
    own, later = total[:half], total[half:]
    terms = [own] + [moved(own, 0, "x", 4, k) for k in range(1, 4)]
    terms += [moved(later, -1, "x", 4, k) for k in range(4)]
    part = latent_call(place, terms)
    part_other = swapped(part)
    ordered = jnp.where(core == 0, jnp.stack([part, part_other]), jnp.stack([part_other, part]))
    latent_grad = ordered.reshape(TOK, PAY)[:, : LATENT + ROPE]
    key_grad, value_grad = weight_call(dw0, dw1)
    return attended, latent_grad, key_grad, value_grad


def solution(mesh):
    split = Mesh(mesh.devices.reshape(GROUPS, 4, 4, 2), ("z", "y", "x", "core"))
    seq, head = ("z", "y"), ("x", "core")
    in_specs = (P(seq, head), P(seq, None), P(seq), P(None, head), P(None, head), P(seq, head))
    out_specs = (P(seq, head), P(seq, None), P(seq, head), P(seq, head))
    return jax.shard_map(
        per_device, mesh=split, in_specs=in_specs, out_specs=out_specs, check_vma=False
    )
```

```python
import functools
import math

import jax
import jax.numpy as jnp
from jax import lax
from jax.experimental import pallas as pl
from jax.experimental.pallas import tpu as pltpu
from jax.sharding import Mesh
from jax.sharding import PartitionSpec as P

NOPE = 128
ROPE = 64
VDIM = 128
LATENT = 512
TOK = 128
ROWS = 4 * TOK
KEYS = 2 * ROWS
TILE = 256
SPAN = ROWS + TILE
PAY = 640
SCALE = 1.0 / math.sqrt(NOPE + ROPE)
LOG2E = math.log2(math.e)
HIDDEN = -1e30
GROUPS = 8
F32 = jnp.float32
BF16 = jnp.bfloat16
SMALL = pltpu.CompilerParams(vmem_limit_bytes=12 << 20)


def nt(a, b):
    return lax.dot_general(a, b, (((1,), (1,)), ((), ())), preferred_element_type=F32)


def nn(a, b):
    return lax.dot_general(a, b, (((1,), (0,)), ((), ())), preferred_element_type=F32)


def tn(a, b):
    return lax.dot_general(a, b, (((0,), (0,)), ((), ())), preferred_element_type=F32)


def pack_kernel(where_ref, q_ref, g_ref, *piece_refs):
    y = where_ref[1]
    for k in range(4):
        to = (y + k) & 3
        for pair in range(2):
            piece = piece_refs[4 * pair + k]
            piece[:, :384] = q_ref[:, pl.ds(pl.multiple_of(to * 768 + pair * 384, 128), 384)]
            piece[:, 384:] = g_ref[:, pl.ds(pl.multiple_of(to * 512 + pair * 256, 128), 256)]


def pack_call(place, queries, out_grad):
    vmem = pl.BlockSpec(memory_space=pltpu.VMEM)
    return pl.pallas_call(
        pack_kernel,
        in_specs=[pl.BlockSpec(memory_space=pltpu.SMEM), vmem, vmem],
        out_specs=[vmem] * 8,
        out_shape=[jax.ShapeDtypeStruct((TOK, PAY), BF16)] * 8,
        cost_estimate=pl.CostEstimate(flops=0, bytes_accessed=2_600_000, transcendentals=0),
        compiler_params=SMALL,
        name="pack",
    )(place, queries, out_grad)


def pair_kernel(first, where_ref, *refs):
    pieces, refs = refs[:4], refs[4:]
    mine_refs, other_refs, refs = refs[:4], refs[4:8], refs[8:]
    wk_ref, wv_ref, refs = refs[0], refs[1], refs[2:]
    if first:
        before_ref, refs = None, refs
        (dl_ref,), outs = refs[:1], refs[1:]
    else:
        before_ref, refs = refs[0], refs[1:]
        keep_ref, send_ref, outs = refs[0], refs[1], refs[2:]
    out_refs, dw_ref = outs[:4], outs[4]
    x_ref, l_ref, kcat, vals, bias, dk_acc, dv_acc, grads, attended, dl_acc = outs[5:]
    group, y, core = where_ref[0], where_ref[1], where_ref[2]
    half = TOK // 2
    for k in range(4):
        block = (y - k) & 3
        x_ref[pl.ds(pl.multiple_of(block * TOK, TOK), TOK), :] = pieces[k][...]
        for back in range(2):
            row = (1 - back) * ROWS + block * TOK
            own = pl.multiple_of(row + core * half, half)
            l_ref[pl.ds(own, half), :] = mine_refs[k][(1 - back) * half : (2 - back) * half]
            swapped = pl.multiple_of(row + (1 - core) * half, half)
            l_ref[pl.ds(swapped, half), :] = other_refs[k][(1 - back) * half : (2 - back) * half]
    lat = l_ref[:, :LATENT]
    tail = l_ref[:, LATENT:].astype(F32)
    lane = lax.broadcasted_iota(jnp.int32, (KEYS, 128), 1)
    low = lane < ROPE

    key_id = tail[:, ROPE : ROPE + 1]
    key_row = lax.broadcasted_iota(jnp.int32, (KEYS, 1), 0)
    key_id = jnp.where((key_row < ROWS) & (group == 0), -1.0, key_id)
    query_id = jnp.transpose(tail[ROWS:])[ROPE : ROPE + 1, :]
    for i in range(2):
        start = i * TILE
        at = lax.broadcasted_iota(jnp.int32, (SPAN, TILE), 0)
        by = lax.broadcasted_iota(jnp.int32, (SPAN, TILE), 1)
        seen = (key_id[start : start + SPAN] == query_id[:, start : start + TILE]) & (
            at <= by + ROWS
        )
        bias[i] = jnp.where(seen, 0.0, HIDDEN)

    keys_up = nn(lat, wk_ref[...])
    vals_up = nn(lat, wv_ref[...])
    vals[...] = vals_up.astype(BF16)
    rope_low = jnp.where(low, tail, 0.0)
    rope_high = pltpu.roll(rope_low, ROPE, 1)
    turned = pltpu.roll(keys_up[:, NOPE:], ROPE, 1)
    kcat[0, :, :NOPE] = keys_up[:, :NOPE].astype(BF16)
    kcat[0, :, NOPE:] = rope_low.astype(BF16)
    kcat[1, :, :NOPE] = jnp.where(low, 0.0, turned).astype(BF16)
    kcat[1, :, NOPE:] = jnp.where(low, turned, rope_high).astype(BF16)

    for h in range(2):
        v_turned = jnp.transpose(vals_up[:, h * VDIM : (h + 1) * VDIM]).astype(BF16)
        for i in range(2):
            start = i * TILE
            span = slice(start, start + SPAN)
            rows = slice(start, start + TILE)
            qc = x_ref[rows, h * NOPE : h * NOPE + 256]
            og = x_ref[rows, 384 + h * VDIM : 384 + (h + 1) * VDIM]
            s = nt(kcat[h, span, :], qc) * (SCALE * LOG2E) + bias[i]
            top = jnp.max(s, axis=0, keepdims=True)
            e = jnp.exp2(s - top)
            p = e * (1.0 / jnp.sum(e, axis=0, keepdims=True))
            pb = p.astype(BF16)
            out_t = nn(v_turned[:, span], pb).astype(BF16).astype(F32)
            attended[rows, h * VDIM : (h + 1) * VDIM] = jnp.transpose(out_t).astype(BF16)
            og_t = jnp.transpose(og.astype(F32))
            delta = jnp.sum(og_t * out_t, axis=0, keepdims=True)
            dp = nn(vals[span, h * VDIM : (h + 1) * VDIM], og_t.astype(BF16))
            ds = (p * (dp - delta) * SCALE).astype(BF16)
            dk = nn(ds, qc)
            dv = nn(pb, og)
            if i == 0:
                dk_acc[h, :SPAN, :] = dk
                dv_acc[:SPAN, :] = dv
            else:
                dk_acc[h, TILE : ROWS + TILE, :] += dk[:ROWS]
                dv_acc[TILE : ROWS + TILE, :] += dv[:ROWS]
                dk_acc[h, SPAN:, :] = dk[ROWS:]
                dv_acc[SPAN:, :] = dv[ROWS:]
        grads[:, 256 + h * VDIM : 256 + (h + 1) * VDIM] = dv_acc[...].astype(BF16)
    for k in range(4):
        to = pl.multiple_of(((y + k) & 3) * TOK, TOK)
        out_refs[k][...] = attended[pl.ds(to, TOK), :]
    grads[:, :NOPE] = dk_acc[0, :, :NOPE].astype(BF16)
    mixed = jnp.where(low, dk_acc[1, :, NOPE:], dk_acc[1, :, :NOPE])
    grads[:, NOPE : 2 * NOPE] = pltpu.roll(mixed, ROPE, 1).astype(BF16)
    rope_grad = jnp.where(low, dk_acc[0, :, NOPE:], dk_acc[1, :, NOPE:])
    rope_grad = rope_grad + pltpu.roll(rope_grad, ROPE, 1)
    dl = nt(grads[:, :256], wk_ref[...]) + nt(grads[:, 256:], wv_ref[...])
    if first:
        dl_ref[:, :LATENT] = dl.astype(BF16)
        dl_ref[:, LATENT:] = rope_grad.astype(BF16)
    else:
        dl_acc[:, :LATENT] = (dl + before_ref[:, :LATENT].astype(F32)).astype(BF16)
        dl_acc[:, LATENT:] = (rope_grad + before_ref[:, LATENT:].astype(F32)).astype(BF16)
        for k in range(4):
            for back in range(2):
                row = (1 - back) * ROWS + ((y + k) & 3) * TOK
                own = pl.multiple_of(row + core * half, half)
                keep_ref[k, back * half : (back + 1) * half, :] = dl_acc[pl.ds(own, half), :]
                swapped = pl.multiple_of(row + (1 - core) * half, half)
                send_ref[k, back * half : (back + 1) * half, :] = dl_acc[pl.ds(swapped, half), :]
    dw_ref[...] = tn(lat, grads[...]).astype(BF16)


def in_hbm(x):
    return pltpu.with_memory_space_constraint(x, pltpu.HBM)


def pair_call(pair, place, pieces, mine, other, key_weight, value_weight, before):
    first = before is None

    def whole(*shape):
        return pl.BlockSpec(shape, lambda i, w: (0,) * len(shape))

    weight_spec = pl.BlockSpec((LATENT, 256), lambda i, w: (0, 2 * w[1] + pair))
    in_specs = [whole(TOK, PAY)] * 12 + [weight_spec] * 2
    args = [in_hbm(x) for x in (*pieces, *mine, *other, key_weight, value_weight)]
    if first:
        dl_shapes = [pltpu.HBM((KEYS, PAY), BF16)]
    else:
        in_specs.append(whole(KEYS, PAY))
        args.append(before)
        dl_shapes = [jax.ShapeDtypeStruct((4, TOK, PAY), BF16)] * 2
    out_shape = dl_shapes + [pltpu.HBM((TOK, 256), BF16)] * 4
    out_shape.append(pltpu.HBM((LATENT, 512), BF16))
    return pl.pallas_call(
        functools.partial(pair_kernel, first),
        grid_spec=pltpu.PrefetchScalarGridSpec(
            num_scalar_prefetch=1,
            grid=(1,),
            in_specs=in_specs,
            out_specs=[whole(*leaf.shape) for leaf in out_shape],
            scratch_shapes=[
                pltpu.VMEM((ROWS, PAY), BF16),
                pltpu.VMEM((KEYS, PAY), BF16),
                pltpu.VMEM((2, KEYS, 256), BF16),
                pltpu.VMEM((KEYS, 256), BF16),
                pltpu.VMEM((2, SPAN, TILE), F32),
                pltpu.VMEM((2, KEYS, 256), F32),
                pltpu.VMEM((KEYS, VDIM), F32),
                pltpu.VMEM((KEYS, 512), BF16),
                pltpu.VMEM((ROWS, 256), BF16),
                pltpu.VMEM((KEYS, PAY), BF16),
            ],
        ),
        out_shape=out_shape,
        compiler_params=pltpu.CompilerParams(vmem_limit_bytes=40 << 20),
        cost_estimate=pl.CostEstimate(
            flops=4_000_000_000, bytes_accessed=8_000_000, transcendentals=800_000
        ),
        name="pair",
    )(place, *args)


def latent_kernel(where_ref, *refs):
    terms, out_ref, held = refs[:4], refs[4], refs[5]
    x = where_ref[3]
    for k in range(4):
        held[(x - k) & 3] = terms[k][...].astype(F32)
    out_ref[...] = (held[0] + held[1]) + (held[2] + held[3])


def latent_call(place, terms):
    vmem = pl.BlockSpec(memory_space=pltpu.VMEM)
    return pl.pallas_call(
        latent_kernel,
        in_specs=[pl.BlockSpec(memory_space=pltpu.SMEM)] + [vmem] * 4,
        out_specs=vmem,
        out_shape=jax.ShapeDtypeStruct((TOK // 2, PAY), F32),
        scratch_shapes=[pltpu.VMEM((4, TOK // 2, PAY), F32)],
        compiler_params=SMALL,
        name="latent",
    )(place, *terms)


def join_kernel(where_ref, mine_ref, other_ref, out_ref):
    first = where_ref[2] == 0
    mine, other = mine_ref[...], other_ref[...]
    rows = jnp.concatenate(
        [jnp.where(first, mine, other), jnp.where(first, other, mine)], axis=0
    )
    out_ref[...] = jnp.transpose(rows)[: LATENT + ROPE]


def join_call(place, mine, other):
    vmem = pl.BlockSpec(memory_space=pltpu.VMEM)
    return pl.pallas_call(
        join_kernel,
        in_specs=[pl.BlockSpec(memory_space=pltpu.SMEM), vmem, vmem],
        out_specs=vmem,
        out_shape=jax.ShapeDtypeStruct((LATENT + ROPE, TOK), F32),
        compiler_params=SMALL,
        name="join",
    )(place, mine, other)


def attended_kernel(where_ref, *refs):
    pieces, out_ref = refs[:8], refs[8]
    y = where_ref[1]
    for pair in range(2):
        for k in range(4):
            column = pl.multiple_of(((y - k) & 3) * 512 + pair * 256, 128)
            out_ref[:, pl.ds(column, 256)] = pieces[4 * pair + k][...]


def attended_call(place, pieces):
    vmem = pl.BlockSpec(memory_space=pltpu.VMEM)
    return pl.pallas_call(
        attended_kernel,
        in_specs=[pl.BlockSpec(memory_space=pltpu.SMEM)] + [vmem] * 8,
        out_specs=vmem,
        out_shape=jax.ShapeDtypeStruct((TOK, 2048), BF16),
        compiler_params=SMALL,
        name="attended",
    )(place, *pieces)


def half_kernel(where_ref, sent_ref, *piece_refs):
    y = where_ref[1]
    for k in range(4):
        row = pl.ds(pl.multiple_of(((y + k) & 3) * 16, 16), 16)
        total = sent_ref[0, row, :].astype(F32)
        for z in range(1, GROUPS):
            total = total + sent_ref[z, row, :].astype(F32)
        piece_refs[k][...] = total.astype(BF16)


def half_call(place, sent):
    vmem = pl.BlockSpec(memory_space=pltpu.VMEM)
    return pl.pallas_call(
        half_kernel,
        in_specs=[pl.BlockSpec(memory_space=pltpu.SMEM), vmem],
        out_specs=[vmem] * 4,
        out_shape=[jax.ShapeDtypeStruct((16, 512), BF16)] * 4,
        compiler_params=SMALL,
        name="half",
    )(place, sent)


def weight_kernel(where_ref, *refs):
    pieces, second_ref, key_ref, value_ref = refs[:4], refs[4], refs[5], refs[6]
    here = where_ref[1]
    for k in range(4):
        column = pl.multiple_of(((here - k) & 3) * 512, 512)
        total = pieces[k][...].astype(F32)
        key_ref[:, pl.ds(column, 256)] = total[:, :256]
        value_ref[:, pl.ds(column, 256)] = total[:, 256:]
    for y in range(4):
        total = second_ref[y].astype(F32)
        for z in range(1, GROUPS):
            total = total + second_ref[4 * z + y].astype(F32)
        column = y * 512 + 256
        key_ref[:, column : column + 256] = total[:, :256]
        value_ref[:, column : column + 256] = total[:, 256:]


def weight_call(place, pieces, second):
    vmem = pl.BlockSpec(memory_space=pltpu.VMEM)
    return pl.pallas_call(
        weight_kernel,
        in_specs=[pl.BlockSpec(memory_space=pltpu.SMEM)] + [vmem] * 5,
        out_specs=[vmem] * 2,
        out_shape=[jax.ShapeDtypeStruct((16, 2048), F32)] * 2,
        compiler_params=SMALL,
        name="weight",
    )(place, *pieces, second)


def exchanged(x, axes):
    return lax.all_to_all(x, axes, split_axis=0, concat_axis=0, tiled=True)


def moved(value, along, size, step):
    return lax.ppermute(value, along, [(i, (i + step) % size) for i in range(size)])


def fanned(pieces, along):
    return [p if k == 0 else moved(p, along, 4, k) for k, p in enumerate(pieces)]


def swapped(value):
    return lax.ppermute(value, "core", [(0, 1), (1, 0)])


def per_device(queries, latents, doc_ids, key_weight, value_weight, out_grad):
    core = lax.axis_index("core")
    place = [lax.axis_index("z"), lax.axis_index("y"), core, lax.axis_index("x")]
    place = jnp.stack(place).astype(jnp.int32)
    half = TOK // 2
    rows = lax.dynamic_slice_in_dim(latents, core * half, half)
    ids = lax.dynamic_slice_in_dim(doc_ids, core * half, half)
    pay = jnp.concatenate(
        [rows, ids.astype(BF16)[:, None], jnp.zeros((half, PAY - 577), BF16)], axis=1
    )
    ahead = [(i, i + 1) for i in range(GROUPS - 1)]
    behind = [(i + 1, i) for i in range(GROUPS - 1)]
    earlier = lax.ppermute(pay, "z", ahead)
    pieces = pack_call(place, queries, out_grad)
    both = jnp.concatenate([earlier, pay], axis=0)
    mine = fanned([both] * 4, "y")
    other = [swapped(piece) for piece in mine]
    x0, x1 = fanned(pieces[:4], "y"), fanned(pieces[4:], "y")

    dl, *outs0, dw0 = pair_call(0, place, x0, mine, other, key_weight, value_weight, None)
    dw0 = half_call(place, exchanged(dw0.reshape(8, 64, 512), "z"))
    keep, send, *outs1, dw1 = pair_call(
        1, place, x1, mine, other, key_weight, value_weight, dl
    )
    dw1 = exchanged(dw1.reshape(32, 16, 512), ("z", "y"))

    came = swapped(send)
    both = [keep[k].astype(F32) + came[k].astype(F32) for k in range(4)]
    parts = fanned([both[0]] + [part.astype(BF16) for part in both[1:]], "y")
    total = parts[0]
    for part in parts[1:]:
        total = total + part.astype(F32)
    later = lax.ppermute(total[half:].astype(BF16), "z", behind)
    later, dw0, outs0, outs1 = lax.optimization_barrier((later, dw0, outs0, outs1))
    own = (total[:half] + later.astype(F32)).astype(BF16)
    part = latent_call(place, fanned([own] * 4, "x"))
    latent_grad = jnp.transpose(join_call(place, part, swapped(part)))
    attended = attended_call(place, fanned(outs0, "y") + fanned(outs1, "y"))
    key_grad, value_grad = weight_call(place, fanned(dw0, "y"), dw1)
    return attended, latent_grad, key_grad, value_grad


def solution(mesh):
    split = Mesh(mesh.devices.reshape(GROUPS, 4, 4, 2), ("z", "y", "x", "core"))
    seq, head = ("z", "y"), ("x", "core")
    in_specs = (P(seq, head), P(seq, None), P(seq), P(None, head), P(None, head), P(seq, head))
    out_specs = (P(seq, head), P(seq, None), P(seq, head), P(seq, head))
    return jax.shard_map(
        per_device, mesh=split, in_specs=in_specs, out_specs=out_specs, check_vma=False
    )
```

```python
import functools
import math

import jax
import jax.numpy as jnp
from jax import lax
from jax.experimental import pallas as pl
from jax.experimental.pallas import tpu as pltpu
from jax.sharding import Mesh
from jax.sharding import PartitionSpec as P

NOPE = 128
ROPE = 64
VDIM = 128
LATENT = 512
TOK = 128
ROWS = 4 * TOK
KEYS = 2 * ROWS
TILE = 256
SPAN = ROWS + TILE
PAY = 640
SCALE = 1.0 / math.sqrt(NOPE + ROPE)
LOG2E = math.log2(math.e)
HIDDEN = -1e30
GROUPS = 8
F32 = jnp.float32
BF16 = jnp.bfloat16
SMALL = pltpu.CompilerParams(vmem_limit_bytes=12 << 20)


def nt(a, b):
    return lax.dot_general(a, b, (((1,), (1,)), ((), ())), preferred_element_type=F32)


def nn(a, b):
    return lax.dot_general(a, b, (((1,), (0,)), ((), ())), preferred_element_type=F32)


def tn(a, b):
    return lax.dot_general(a, b, (((0,), (0,)), ((), ())), preferred_element_type=F32)


def in_hbm(x):
    return pltpu.with_memory_space_constraint(x, pltpu.HBM)


def pack_kernel(q_ref, g_ref, earlier_ref, own_ref, out_ref):
    for pair in range(2):
        rows = slice(pair * TOK, (pair + 1) * TOK)
        out_ref[0, rows, :384] = q_ref[:, pair * 384 : (pair + 1) * 384]
        out_ref[0, rows, 384:] = g_ref[:, pair * 256 : (pair + 1) * 256]
    out_ref[0, 2 * TOK : 2 * TOK + TOK // 2, :] = earlier_ref[...]
    out_ref[0, 2 * TOK + TOK // 2 :, :] = own_ref[...]


def pack_call(queries, out_grad, earlier, own):
    half = pl.BlockSpec((TOK // 2, PAY), lambda y: (0, 0))
    return pl.pallas_call(
        pack_kernel,
        grid=(4,),
        in_specs=[
            pl.BlockSpec((TOK, 768), lambda y: (0, y)),
            pl.BlockSpec((TOK, 512), lambda y: (0, y)),
            half,
            half,
        ],
        out_specs=pl.BlockSpec((1, 3 * TOK, PAY), lambda y: (y, 0, 0)),
        out_shape=pltpu.HBM((4, 3 * TOK, PAY), BF16),
        cost_estimate=pl.CostEstimate(flops=0, bytes_accessed=3_300_000, transcendentals=0),
        compiler_params=SMALL,
        name="pack",
    )(in_hbm(queries), in_hbm(out_grad), earlier, own)


def pair_kernel(where_ref, x_ref, mine_ref, other_ref, wk_ref, wv_ref, *refs):
    keep_ref, send_ref, out_refs, dw_ref = refs[0], refs[1], refs[2:6], refs[6]
    l_ref, kcat, vals, bias, dk_acc, dv_acc, grads, attended, dl_acc = refs[7:]
    group, y, core = where_ref[0], where_ref[1], where_ref[2]
    pair = pl.program_id(0)
    half = TOK // 2
    lane = lax.broadcasted_iota(jnp.int32, (KEYS, 128), 1)
    low = lane < ROPE

    @pl.when(pair == 0)
    def _():
        for block in range(4):
            for own in range(2):
                row = own * ROWS + block * TOK
                piece = slice(own * half, (own + 1) * half)
                at = pl.multiple_of(row + core * half, half)
                l_ref[pl.ds(at, half), :] = mine_ref[block, piece]
                at = pl.multiple_of(row + (1 - core) * half, half)
                l_ref[pl.ds(at, half), :] = other_ref[block, piece]
        ids = l_ref[:, LATENT:].astype(F32)
        key_id = ids[:, ROPE : ROPE + 1]
        key_row = lax.broadcasted_iota(jnp.int32, (KEYS, 1), 0)
        key_id = jnp.where((key_row < ROWS) & (group == 0), -1.0, key_id)
        query_id = jnp.transpose(ids[ROWS:])[ROPE : ROPE + 1, :]
        for i in range(2):
            start = i * TILE
            at = lax.broadcasted_iota(jnp.int32, (SPAN, TILE), 0)
            by = lax.broadcasted_iota(jnp.int32, (SPAN, TILE), 1)
            seen = (key_id[start : start + SPAN] == query_id[:, start : start + TILE]) & (
                at <= by + ROWS
            )
            bias[i] = jnp.where(seen, 0.0, HIDDEN)

    lat = l_ref[:, :LATENT]
    tail = l_ref[:, LATENT:].astype(F32)
    keys_up = nn(lat, wk_ref[...])
    vals_up = nn(lat, wv_ref[...])
    vals[...] = vals_up.astype(BF16)
    rope_low = jnp.where(low, tail, 0.0)
    rope_high = pltpu.roll(rope_low, ROPE, 1)
    turned = pltpu.roll(keys_up[:, NOPE:], ROPE, 1)
    kcat[0, :, :NOPE] = keys_up[:, :NOPE].astype(BF16)
    kcat[0, :, NOPE:] = rope_low.astype(BF16)
    kcat[1, :, :NOPE] = jnp.where(low, 0.0, turned).astype(BF16)
    kcat[1, :, NOPE:] = jnp.where(low, turned, rope_high).astype(BF16)

    for h in range(2):
        v_turned = jnp.transpose(vals_up[:, h * VDIM : (h + 1) * VDIM]).astype(BF16)
        for i in range(2):
            start = i * TILE
            span = slice(start, start + SPAN)
            rows = slice(start, start + TILE)
            qc = x_ref[2 * i : 2 * i + 2, :, h * NOPE : h * NOPE + 256].reshape(TILE, 256)
            og = x_ref[2 * i : 2 * i + 2, :, 384 + h * VDIM : 384 + (h + 1) * VDIM]
            og = og.reshape(TILE, VDIM)
            s = nt(kcat[h, span, :], qc) * (SCALE * LOG2E) + bias[i]
            top = jnp.max(s, axis=0, keepdims=True)
            e = jnp.exp2(s - top)
            p = e * (1.0 / jnp.sum(e, axis=0, keepdims=True))
            pb = p.astype(BF16)
            out_t = nn(v_turned[:, span], pb).astype(BF16).astype(F32)
            attended[rows, h * VDIM : (h + 1) * VDIM] = jnp.transpose(out_t).astype(BF16)
            og_t = jnp.transpose(og.astype(F32))
            delta = jnp.sum(og_t * out_t, axis=0, keepdims=True)
            dp = nn(vals[span, h * VDIM : (h + 1) * VDIM], og_t.astype(BF16))
            ds = (p * (dp - delta) * SCALE).astype(BF16)
            dk = nn(ds, qc)
            dv = nn(pb, og)
            if i == 0:
                dk_acc[h, :SPAN, :] = dk
                dv_acc[:SPAN, :] = dv
            else:
                dk_acc[h, TILE : ROWS + TILE, :] += dk[:ROWS]
                dv_acc[TILE : ROWS + TILE, :] += dv[:ROWS]
                dk_acc[h, SPAN:, :] = dk[ROWS:]
                dv_acc[SPAN:, :] = dv[ROWS:]
        grads[:, 256 + h * VDIM : 256 + (h + 1) * VDIM] = dv_acc[...].astype(BF16)
    column = pl.ds(pl.multiple_of(pair * 256, 256), 256)
    for k in range(4):
        to = pl.multiple_of(((y + k) & 3) * TOK, TOK)
        out_refs[k][:, column] = attended[pl.ds(to, TOK), :]
    grads[:, :NOPE] = dk_acc[0, :, :NOPE].astype(BF16)
    mixed = jnp.where(low, dk_acc[1, :, NOPE:], dk_acc[1, :, :NOPE])
    grads[:, NOPE : 2 * NOPE] = pltpu.roll(mixed, ROPE, 1).astype(BF16)
    rope_grad = jnp.where(low, dk_acc[0, :, NOPE:], dk_acc[1, :, NOPE:])
    rope_grad = rope_grad + pltpu.roll(rope_grad, ROPE, 1)
    dl = nt(grads[:, :256], wk_ref[...]) + nt(grads[:, 256:], wv_ref[...])
    dw_ref[...] = tn(lat, grads[...]).astype(BF16)

    @pl.when(pair == 0)
    def _():
        dl_acc[:, :LATENT] = dl
        dl_acc[:, LATENT:] = rope_grad

    @pl.when(pair == 1)
    def _():
        dl_acc[:, :LATENT] += dl
        dl_acc[:, LATENT:] += rope_grad
        for k in range(4):
            for back in range(2):
                row = (1 - back) * ROWS + ((y + k) & 3) * TOK
                piece = slice(back * half, (back + 1) * half)
                at = pl.multiple_of(row + core * half, half)
                keep_ref[k, piece, :] = dl_acc[pl.ds(at, half), :].astype(BF16)
                at = pl.multiple_of(row + (1 - core) * half, half)
                send_ref[k, piece, :] = dl_acc[pl.ds(at, half), :].astype(BF16)


def pair_call(place, x, other, key_weight, value_weight):
    def whole(*shape):
        return pl.BlockSpec(shape, lambda i, w: (0,) * len(shape))

    weight_spec = pl.BlockSpec((LATENT, 256), lambda i, w: (0, 2 * w[1] + i))
    x_spec = pl.BlockSpec((4, TOK, PAY), lambda i, w: (0, i, 0))
    lat_spec = pl.BlockSpec((4, TOK, PAY), lambda i, w: (0, 2, 0))
    dw_spec = pl.BlockSpec((LATENT, 512), lambda i, w: (0, i))
    return pl.pallas_call(
        pair_kernel,
        grid_spec=pltpu.PrefetchScalarGridSpec(
            num_scalar_prefetch=1,
            grid=(2,),
            in_specs=[x_spec, lat_spec, whole(4, TOK, PAY), weight_spec, weight_spec],
            out_specs=[whole(4, TOK, PAY)] * 2 + [whole(TOK, 512)] * 4 + [dw_spec],
            scratch_shapes=[
                pltpu.VMEM((KEYS, PAY), BF16),
                pltpu.VMEM((2, KEYS, 256), BF16),
                pltpu.VMEM((KEYS, 256), BF16),
                pltpu.VMEM((2, SPAN, TILE), F32),
                pltpu.VMEM((2, KEYS, 256), F32),
                pltpu.VMEM((KEYS, VDIM), F32),
                pltpu.VMEM((KEYS, 512), BF16),
                pltpu.VMEM((ROWS, 256), BF16),
                pltpu.VMEM((KEYS, PAY), F32),
            ],
        ),
        out_shape=[pltpu.HBM((4, TOK, PAY), BF16)] * 2
        + [pltpu.HBM((TOK, 512), BF16)] * 4
        + [pltpu.HBM((LATENT, 1024), BF16)],
        compiler_params=pltpu.CompilerParams(vmem_limit_bytes=40 << 20),
        cost_estimate=pl.CostEstimate(
            flops=8_000_000_000, bytes_accessed=10_000_000, transcendentals=1_600_000
        ),
        name="pair",
    )(place, in_hbm(x), in_hbm(x), in_hbm(other), in_hbm(key_weight), in_hbm(value_weight))


def latent_kernel(where_ref, *refs):
    terms, out_ref, held = refs[:4], refs[4], refs[5]
    x = where_ref[3]
    for k in range(4):
        held[(x - k) & 3] = terms[k][...].astype(F32)
    out_ref[...] = (held[0] + held[1]) + (held[2] + held[3])


def latent_call(place, terms):
    vmem = pl.BlockSpec(memory_space=pltpu.VMEM)
    return pl.pallas_call(
        latent_kernel,
        in_specs=[pl.BlockSpec(memory_space=pltpu.SMEM)] + [vmem] * 4,
        out_specs=vmem,
        out_shape=jax.ShapeDtypeStruct((TOK // 2, PAY), F32),
        scratch_shapes=[pltpu.VMEM((4, TOK // 2, PAY), F32)],
        compiler_params=SMALL,
        name="latent",
    )(place, *terms)


def join_kernel(where_ref, mine_ref, other_ref, out_ref):
    first = where_ref[2] == 0
    mine, other = mine_ref[...], other_ref[...]
    rows = jnp.concatenate(
        [jnp.where(first, mine, other), jnp.where(first, other, mine)], axis=0
    )
    out_ref[...] = jnp.transpose(rows)[: LATENT + ROPE]


def join_call(place, mine, other):
    vmem = pl.BlockSpec(memory_space=pltpu.VMEM)
    return pl.pallas_call(
        join_kernel,
        in_specs=[pl.BlockSpec(memory_space=pltpu.SMEM), vmem, vmem],
        out_specs=vmem,
        out_shape=jax.ShapeDtypeStruct((LATENT + ROPE, TOK), F32),
        compiler_params=SMALL,
        name="join",
    )(place, mine, other)


def attended_kernel(where_ref, *refs):
    pieces, out_ref = refs[:4], refs[4]
    y = where_ref[1]
    for k in range(4):
        column = pl.multiple_of(((y - k) & 3) * 512, 512)
        out_ref[:, pl.ds(column, 512)] = pieces[k][...]


def attended_call(place, pieces):
    vmem = pl.BlockSpec(memory_space=pltpu.VMEM)
    return pl.pallas_call(
        attended_kernel,
        in_specs=[pl.BlockSpec(memory_space=pltpu.SMEM)] + [vmem] * 4,
        out_specs=vmem,
        out_shape=jax.ShapeDtypeStruct((TOK, 2048), BF16),
        compiler_params=SMALL,
        name="attended",
    )(place, *pieces)


def half_kernel(where_ref, sent_ref, *piece_refs):
    y = where_ref[1]
    for k in range(4):
        row = pl.ds(pl.multiple_of(((y + k) & 3) * 16, 16), 16)
        total = sent_ref[0, row, :].astype(F32)
        for z in range(1, GROUPS):
            total = total + sent_ref[z, row, :].astype(F32)
        piece_refs[k][...] = total.astype(BF16)


def half_call(place, sent):
    vmem = pl.BlockSpec(memory_space=pltpu.VMEM)
    return pl.pallas_call(
        half_kernel,
        in_specs=[pl.BlockSpec(memory_space=pltpu.SMEM), vmem],
        out_specs=[vmem] * 4,
        out_shape=[jax.ShapeDtypeStruct((16, 1024), BF16)] * 4,
        compiler_params=SMALL,
        name="half",
    )(place, sent)


def weight_kernel(where_ref, *refs):
    pieces, key_ref, value_ref = refs[:4], refs[4], refs[5]
    y = where_ref[1]
    for k in range(4):
        column = ((y - k) & 3) * 512
        for pair in range(2):
            here = pl.ds(pl.multiple_of(column + pair * 256, 256), 256)
            key_ref[:, here] = pieces[k][:, pair * 512 : pair * 512 + 256].astype(F32)
            value_ref[:, here] = pieces[k][:, pair * 512 + 256 : pair * 512 + 512].astype(F32)


def weight_call(place, pieces):
    vmem = pl.BlockSpec(memory_space=pltpu.VMEM)
    return pl.pallas_call(
        weight_kernel,
        in_specs=[pl.BlockSpec(memory_space=pltpu.SMEM)] + [vmem] * 4,
        out_specs=[vmem] * 2,
        out_shape=[jax.ShapeDtypeStruct((16, 2048), F32)] * 2,
        compiler_params=SMALL,
        name="weight",
    )(place, *pieces)


def exchanged(x, axes):
    return lax.all_to_all(x, axes, split_axis=0, concat_axis=0, tiled=True)


def moved(value, along, size, step):
    return lax.ppermute(value, along, [(i, (i + step) % size) for i in range(size)])


def fanned(pieces, along):
    return [p if k == 0 else moved(p, along, 4, k) for k, p in enumerate(pieces)]


def swapped(value):
    return lax.ppermute(value, "core", [(0, 1), (1, 0)])


def per_device(queries, latents, doc_ids, key_weight, value_weight, out_grad):
    core = lax.axis_index("core")
    place = [lax.axis_index("z"), lax.axis_index("y"), core, lax.axis_index("x")]
    place = jnp.stack(place).astype(jnp.int32)
    half = TOK // 2
    rows = lax.dynamic_slice_in_dim(latents, core * half, half)
    ids = lax.dynamic_slice_in_dim(doc_ids, core * half, half)
    pay = jnp.concatenate(
        [rows, ids.astype(BF16)[:, None], jnp.zeros((half, PAY - 577), BF16)], axis=1
    )
    ahead = [(i, i + 1) for i in range(GROUPS - 1)]
    behind = [(i + 1, i) for i in range(GROUPS - 1)]
    earlier = lax.ppermute(pay, "z", ahead)
    x = exchanged(pack_call(queries, out_grad, earlier, pay), "y")
    other = swapped(x[:, 2 * TOK :])
    keep, send, *outs, dw = pair_call(place, x, other, key_weight, value_weight)

    came = swapped(send)
    dw = half_call(place, exchanged(dw.reshape(8, 64, 1024), "z"))
    both = [keep[k].astype(F32) + came[k].astype(F32) for k in range(4)]
    parts = fanned([both[0]] + [part.astype(BF16) for part in both[1:]], "y")
    total = parts[0]
    for part in parts[1:]:
        total = total + part.astype(F32)
    later, outs = lax.optimization_barrier((total[half:].astype(BF16), outs))
    later = lax.ppermute(later, "z", behind)
    own = (total[:half] + later.astype(F32)).astype(BF16)
    part = latent_call(place, fanned([own] * 4, "x"))
    latent_grad = jnp.transpose(join_call(place, part, swapped(part)))
    attended = attended_call(place, fanned(outs, "y"))
    key_grad, value_grad = weight_call(place, fanned(dw, "y"))
    return attended, latent_grad, key_grad, value_grad


def solution(mesh):
    split = Mesh(mesh.devices.reshape(GROUPS, 4, 4, 2), ("z", "y", "x", "core"))
    seq, head = ("z", "y"), ("x", "core")
    in_specs = (P(seq, head), P(seq, None), P(seq), P(None, head), P(None, head), P(seq, head))
    out_specs = (P(seq, head), P(seq, None), P(seq, head), P(seq, head))
    return jax.shard_map(
        per_device, mesh=split, in_specs=in_specs, out_specs=out_specs, check_vma=False
    )
```

```python
import functools
import math

import jax
import jax.numpy as jnp
from jax import lax
from jax.experimental import pallas as pl
from jax.experimental.pallas import tpu as pltpu
from jax.sharding import Mesh
from jax.sharding import PartitionSpec as P

NOPE = 128
ROPE = 64
VDIM = 128
LATENT = 512
TOK = 128
ROWS = 4 * TOK
KEYS = 2 * ROWS
TILE = 256
SPAN = ROWS + TILE
PAY = 640
SCALE = 1.0 / math.sqrt(NOPE + ROPE)
LOG2E = math.log2(math.e)
HIDDEN = -1e30
GROUPS = 8
F32 = jnp.float32
BF16 = jnp.bfloat16
SMALL = pltpu.CompilerParams(vmem_limit_bytes=12 << 20)


def nt(a, b):
    return lax.dot_general(a, b, (((1,), (1,)), ((), ())), preferred_element_type=F32)


def nn(a, b):
    return lax.dot_general(a, b, (((1,), (0,)), ((), ())), preferred_element_type=F32)


def tn(a, b):
    return lax.dot_general(a, b, (((0,), (0,)), ((), ())), preferred_element_type=F32)


def in_hbm(x):
    return pltpu.with_memory_space_constraint(x, pltpu.HBM)


def pack_kernel(where_ref, q_ref, g_ref, *refs):
    piece_refs, sems = refs[:8], refs[8]
    y = where_ref[1]
    copies = []
    for pair in range(2):
        for k in range(4):
            to = (y + k) & 3
            piece = piece_refs[4 * pair + k]
            from_q = q_ref.at[:, pl.ds(pl.multiple_of(to * 768 + pair * 384, 128), 384)]
            from_g = g_ref.at[:, pl.ds(pl.multiple_of(to * 512 + pair * 256, 128), 256)]
            at = 8 * pair + 2 * k
            copies.append(pltpu.make_async_copy(from_q, piece.at[:, :384], sems.at[at]))
            copies.append(pltpu.make_async_copy(from_g, piece.at[:, 384:], sems.at[at + 1]))
    for copy in copies:
        copy.start()
    for copy in copies:
        copy.wait()


def pack_call(place, queries, out_grad):
    hbm = pl.BlockSpec(memory_space=pltpu.HBM)
    return pl.pallas_call(
        pack_kernel,
        in_specs=[pl.BlockSpec(memory_space=pltpu.SMEM), hbm, hbm],
        out_specs=[hbm] * 8,
        out_shape=[pltpu.HBM((TOK, PAY), BF16)] * 8,
        scratch_shapes=[pltpu.SemaphoreType.DMA((16,))],
        cost_estimate=pl.CostEstimate(flops=0, bytes_accessed=2_600_000, transcendentals=0),
        compiler_params=SMALL,
        name="pack",
    )(place, in_hbm(queries), in_hbm(out_grad))


def pair_kernel(first, where_ref, *refs):
    pieces, refs = refs[:4], refs[4:]
    if first:
        mine_refs, other_refs, refs = refs[:4], refs[4:8], refs[8:]
        wk_ref, wv_ref, l_ref, dl_ref, attended, grads = refs[:6]
    else:
        l_ref, wk_ref, wv_ref, before_ref, early_ref, refs = *refs[:5], refs[5:]
        keep_ref, send_ref, out_refs, grads, refs = refs[0], refs[1], refs[2:6], refs[6], refs[7:]
        attended, dl_acc = refs[-2:]
    x_ref, kcat, vals, bias, dk_acc, dv_acc = refs[6:12] if first else refs[:6]
    group, y, core = where_ref[0], where_ref[1], where_ref[2]
    half = TOK // 2
    for k in range(4):
        block = (y - k) & 3
        x_ref[pl.ds(pl.multiple_of(block * TOK, TOK), TOK), :] = pieces[k][...]
        for back in range(2):
            if not first:
                continue
            row = (1 - back) * ROWS + block * TOK
            piece = slice((1 - back) * half, (2 - back) * half)
            own = pl.multiple_of(row + core * half, half)
            l_ref[pl.ds(own, half), :] = mine_refs[k][piece]
            swapped = pl.multiple_of(row + (1 - core) * half, half)
            l_ref[pl.ds(swapped, half), :] = other_refs[k][piece]
    lat = l_ref[:, :LATENT]
    tail = l_ref[:, LATENT:].astype(F32)
    lane = lax.broadcasted_iota(jnp.int32, (KEYS, 128), 1)
    low = lane < ROPE

    key_id = tail[:, ROPE : ROPE + 1]
    key_row = lax.broadcasted_iota(jnp.int32, (KEYS, 1), 0)
    key_id = jnp.where((key_row < ROWS) & (group == 0), -1.0, key_id)
    query_id = jnp.transpose(tail[ROWS:])[ROPE : ROPE + 1, :]
    for i in range(2):
        start = i * TILE
        at = lax.broadcasted_iota(jnp.int32, (SPAN, TILE), 0)
        by = lax.broadcasted_iota(jnp.int32, (SPAN, TILE), 1)
        seen = (key_id[start : start + SPAN] == query_id[:, start : start + TILE]) & (
            at <= by + ROWS
        )
        bias[i] = jnp.where(seen, 0.0, HIDDEN)

    keys_up = nn(lat, wk_ref[...])
    vals_up = nn(lat, wv_ref[...])
    vals[...] = vals_up.astype(BF16)
    rope_low = jnp.where(low, tail, 0.0)
    rope_high = pltpu.roll(rope_low, ROPE, 1)
    turned = pltpu.roll(keys_up[:, NOPE:], ROPE, 1)
    kcat[0, :, :NOPE] = keys_up[:, :NOPE].astype(BF16)
    kcat[0, :, NOPE:] = rope_low.astype(BF16)
    kcat[1, :, :NOPE] = jnp.where(low, 0.0, turned).astype(BF16)
    kcat[1, :, NOPE:] = jnp.where(low, turned, rope_high).astype(BF16)

    for h in range(2):
        v_turned = jnp.transpose(vals_up[:, h * VDIM : (h + 1) * VDIM]).astype(BF16)
        for i in range(2):
            start = i * TILE
            span = slice(start, start + SPAN)
            rows = slice(start, start + TILE)
            qc = x_ref[rows, h * NOPE : h * NOPE + 256]
            og = x_ref[rows, 384 + h * VDIM : 384 + (h + 1) * VDIM]
            s = nt(kcat[h, span, :], qc) * (SCALE * LOG2E) + bias[i]
            top = jnp.max(s, axis=0, keepdims=True)
            e = jnp.exp2(s - top)
            p = e * (1.0 / jnp.sum(e, axis=0, keepdims=True))
            pb = p.astype(BF16)
            out_t = nn(v_turned[:, span], pb).astype(BF16).astype(F32)
            attended[rows, h * VDIM : (h + 1) * VDIM] = jnp.transpose(out_t).astype(BF16)
            og_t = jnp.transpose(og.astype(F32))
            delta = jnp.sum(og_t * out_t, axis=0, keepdims=True)
            dp = nn(vals[span, h * VDIM : (h + 1) * VDIM], og_t.astype(BF16))
            ds = (p * (dp - delta) * SCALE).astype(BF16)
            dk = nn(ds, qc)
            dv = nn(pb, og)
            if i == 0:
                dk_acc[h, :SPAN, :] = dk
                dv_acc[:SPAN, :] = dv
            else:
                dk_acc[h, TILE : ROWS + TILE, :] += dk[:ROWS]
                dv_acc[TILE : ROWS + TILE, :] += dv[:ROWS]
                dk_acc[h, SPAN:, :] = dk[ROWS:]
                dv_acc[SPAN:, :] = dv[ROWS:]
        grads[:, 256 + h * VDIM : 256 + (h + 1) * VDIM] = dv_acc[...].astype(BF16)
    if not first:
        for k in range(4):
            to = pl.multiple_of(((y + k) & 3) * TOK, TOK)
            out_refs[k][:, :256] = early_ref[pl.ds(to, TOK), :]
            out_refs[k][:, 256:] = attended[pl.ds(to, TOK), :]
    grads[:, :NOPE] = dk_acc[0, :, :NOPE].astype(BF16)
    mixed = jnp.where(low, dk_acc[1, :, NOPE:], dk_acc[1, :, :NOPE])
    grads[:, NOPE : 2 * NOPE] = pltpu.roll(mixed, ROPE, 1).astype(BF16)
    rope_grad = jnp.where(low, dk_acc[0, :, NOPE:], dk_acc[1, :, NOPE:])
    rope_grad = rope_grad + pltpu.roll(rope_grad, ROPE, 1)
    dl = nt(grads[:, :256], wk_ref[...]) + nt(grads[:, 256:], wv_ref[...])
    if first:
        dl_ref[:, :LATENT] = dl.astype(BF16)
        dl_ref[:, LATENT:] = rope_grad.astype(BF16)
    else:
        dl_acc[:, :LATENT] = (dl + before_ref[:, :LATENT].astype(F32)).astype(BF16)
        dl_acc[:, LATENT:] = (rope_grad + before_ref[:, LATENT:].astype(F32)).astype(BF16)
        for k in range(4):
            for back in range(2):
                row = (1 - back) * ROWS + ((y + k) & 3) * TOK
                own = pl.multiple_of(row + core * half, half)
                keep_ref[k, back * half : (back + 1) * half, :] = dl_acc[pl.ds(own, half), :]
                swapped = pl.multiple_of(row + (1 - core) * half, half)
                send_ref[k, back * half : (back + 1) * half, :] = dl_acc[pl.ds(swapped, half), :]


def pair_call(pair, place, pieces, lats, key_weight, value_weight, before):
    first = pair == 0

    def whole(*shape):
        return pl.BlockSpec(shape, lambda i, w: (0,) * len(shape))

    weight_spec = pl.BlockSpec((LATENT, 256), lambda i, w: (0, 2 * w[1] + pair))
    args = [*pieces, *lats]
    in_specs = [whole(*arg.shape) for arg in args] + [weight_spec] * 2
    in_specs += [whole(*arg.shape) for arg in before]
    scratch = [
        pltpu.VMEM((ROWS, PAY), BF16),
        pltpu.VMEM((2, KEYS, 256), BF16),
        pltpu.VMEM((KEYS, 256), BF16),
        pltpu.VMEM((2, SPAN, TILE), F32),
        pltpu.VMEM((2, KEYS, 256), F32),
        pltpu.VMEM((KEYS, VDIM), F32),
    ]
    grads = pltpu.HBM((KEYS, 512), BF16)
    if first:
        out_shape = [pltpu.HBM((KEYS, PAY), BF16)] * 2 + [pltpu.HBM((ROWS, 256), BF16), grads]
    else:
        out_shape = [pltpu.HBM((4, TOK, PAY), BF16)] * 2
        out_shape += [pltpu.HBM((TOK, 512), BF16)] * 4 + [grads]
        scratch += [pltpu.VMEM((ROWS, 256), BF16), pltpu.VMEM((KEYS, PAY), BF16)]
    args += [in_hbm(arg) for arg in (key_weight, value_weight, *before)]
    return pl.pallas_call(
        functools.partial(pair_kernel, first),
        grid_spec=pltpu.PrefetchScalarGridSpec(
            num_scalar_prefetch=1,
            grid=(1,),
            in_specs=in_specs,
            out_specs=[whole(*leaf.shape) for leaf in out_shape],
            scratch_shapes=scratch,
        ),
        out_shape=out_shape,
        compiler_params=pltpu.CompilerParams(vmem_limit_bytes=40 << 20),
        cost_estimate=pl.CostEstimate(
            flops=4_000_000_000, bytes_accessed=8_000_000, transcendentals=800_000
        ),
        name="pair",
    )(place, *args)


def grad_kernel(l_ref, first_ref, second_ref, out_ref):
    lat_t = jnp.transpose(l_ref[:, :LATENT])
    out_ref[:, :512] = nn(lat_t, first_ref[...]).astype(BF16)
    out_ref[:, 512:] = nn(lat_t, second_ref[...]).astype(BF16)


def grad_call(lat, first, second):
    vmem = pl.BlockSpec(memory_space=pltpu.VMEM)
    return pl.pallas_call(
        grad_kernel,
        in_specs=[vmem] * 3,
        out_specs=vmem,
        out_shape=pltpu.HBM((LATENT, 1024), BF16),
        compiler_params=pltpu.CompilerParams(vmem_limit_bytes=20 << 20),
        cost_estimate=pl.CostEstimate(
            flops=1_100_000_000, bytes_accessed=4_400_000, transcendentals=0
        ),
        name="grad",
    )(in_hbm(lat), in_hbm(first), in_hbm(second))


def latent_kernel(where_ref, *refs):
    terms, own_ref, later_ref, held = refs[:4], refs[4], refs[5], refs[6]
    x = where_ref[3]
    for k in range(4):
        held[(x - k) & 3] = terms[k][...].astype(F32)
    total = (held[0] + held[1]) + (held[2] + held[3])
    own_ref[...] = total[: TOK // 2]
    later_ref[...] = total[TOK // 2 :].astype(BF16)


def latent_call(place, terms):
    vmem = pl.BlockSpec(memory_space=pltpu.VMEM)
    return pl.pallas_call(
        latent_kernel,
        in_specs=[pl.BlockSpec(memory_space=pltpu.SMEM)] + [vmem] * 4,
        out_specs=[vmem] * 2,
        out_shape=[
            jax.ShapeDtypeStruct((TOK // 2, PAY), F32),
            jax.ShapeDtypeStruct((TOK // 2, PAY), BF16),
        ],
        scratch_shapes=[pltpu.VMEM((4, TOK, PAY), F32)],
        compiler_params=SMALL,
        name="latent",
    )(place, *terms)


def join_kernel(where_ref, mine_ref, other_ref, out_ref):
    first = where_ref[2] == 0
    mine, other = mine_ref[...], other_ref[...]
    rows = jnp.concatenate(
        [jnp.where(first, mine, other), jnp.where(first, other, mine)], axis=0
    )
    out_ref[...] = jnp.transpose(rows)[: LATENT + ROPE]


def join_call(place, mine, other):
    vmem = pl.BlockSpec(memory_space=pltpu.VMEM)
    return pl.pallas_call(
        join_kernel,
        in_specs=[pl.BlockSpec(memory_space=pltpu.SMEM), vmem, vmem],
        out_specs=vmem,
        out_shape=jax.ShapeDtypeStruct((LATENT + ROPE, TOK), F32),
        compiler_params=SMALL,
        name="join",
    )(place, mine, other)


def attended_kernel(where_ref, *refs):
    pieces, out_ref = refs[:4], refs[4]
    y = where_ref[1]
    for k in range(4):
        column = pl.multiple_of(((y - k) & 3) * 512, 512)
        out_ref[:, pl.ds(column, 512)] = pieces[k][...]


def attended_call(place, pieces):
    vmem = pl.BlockSpec(memory_space=pltpu.VMEM)
    return pl.pallas_call(
        attended_kernel,
        in_specs=[pl.BlockSpec(memory_space=pltpu.SMEM)] + [vmem] * 4,
        out_specs=vmem,
        out_shape=jax.ShapeDtypeStruct((TOK, 2048), BF16),
        compiler_params=SMALL,
        name="attended",
    )(place, *pieces)


def half_kernel(where_ref, sent_ref, *piece_refs):
    y = where_ref[1]
    for k in range(4):
        row = pl.ds(pl.multiple_of(((y + k) & 3) * 16, 16), 16)
        total = sent_ref[0, row, :].astype(F32)
        for z in range(1, GROUPS):
            total = total + sent_ref[z, row, :].astype(F32)
        piece_refs[k][...] = total.astype(BF16)


def half_call(place, sent):
    vmem = pl.BlockSpec(memory_space=pltpu.VMEM)
    return pl.pallas_call(
        half_kernel,
        in_specs=[pl.BlockSpec(memory_space=pltpu.SMEM), vmem],
        out_specs=[vmem] * 4,
        out_shape=[jax.ShapeDtypeStruct((16, 1024), BF16)] * 4,
        compiler_params=SMALL,
        name="half",
    )(place, sent)


def weight_kernel(where_ref, *refs):
    pieces, key_ref, value_ref = refs[:4], refs[4], refs[5]
    y = where_ref[1]
    for k in range(4):
        column = ((y - k) & 3) * 512
        for pair in range(2):
            here = pl.ds(pl.multiple_of(column + pair * 256, 256), 256)
            key_ref[:, here] = pieces[k][:, pair * 512 : pair * 512 + 256].astype(F32)
            value_ref[:, here] = pieces[k][:, pair * 512 + 256 : pair * 512 + 512].astype(F32)


def weight_call(place, pieces):
    vmem = pl.BlockSpec(memory_space=pltpu.VMEM)
    return pl.pallas_call(
        weight_kernel,
        in_specs=[pl.BlockSpec(memory_space=pltpu.SMEM)] + [vmem] * 4,
        out_specs=[vmem] * 2,
        out_shape=[jax.ShapeDtypeStruct((16, 2048), F32)] * 2,
        compiler_params=SMALL,
        name="weight",
    )(place, *pieces)


def exchanged(x, axes):
    return lax.all_to_all(x, axes, split_axis=0, concat_axis=0, tiled=True)


def moved(value, along, size, step):
    return lax.ppermute(value, along, [(i, (i + step) % size) for i in range(size)])


def fanned(pieces, along):
    return [p if k == 0 else moved(p, along, 4, k) for k, p in enumerate(pieces)]


def swapped(value):
    return lax.ppermute(value, "core", [(0, 1), (1, 0)])


def per_device(queries, latents, doc_ids, key_weight, value_weight, out_grad):
    core = lax.axis_index("core")
    place = [lax.axis_index("z"), lax.axis_index("y"), core, lax.axis_index("x")]
    place = jnp.stack(place).astype(jnp.int32)
    half = TOK // 2
    rows = lax.dynamic_slice_in_dim(latents, core * half, half)
    ids = lax.dynamic_slice_in_dim(doc_ids, core * half, half)
    pay = jnp.concatenate(
        [rows, ids.astype(BF16)[:, None], jnp.zeros((half, PAY - 577), BF16)], axis=1
    )
    ahead = [(i, i + 1) for i in range(GROUPS - 1)]
    behind = [(i + 1, i) for i in range(GROUPS - 1)]
    earlier = lax.ppermute(pay, "z", ahead)
    pieces = pack_call(place, queries, out_grad)
    both = jnp.concatenate([earlier, pay], axis=0)
    mine = fanned([both] * 4, "y")
    other = [swapped(piece) for piece in mine]
    x0, x1 = fanned(pieces[:4], "y"), fanned(pieces[4:], "y")

    lat, dl, early, g0 = pair_call(0, place, x0, mine + other, key_weight, value_weight, [])
    keep, send, *outs, g1 = pair_call(1, place, x1, [lat], key_weight, value_weight, [dl, early])

    came = swapped(send)
    both = [keep[k].astype(F32) + came[k].astype(F32) for k in range(4)]
    both = [both[0]] + [part.astype(BF16) for part in both[1:]]
    both, g1 = lax.optimization_barrier((both, g1))
    parts = fanned(both, "y")
    dw = exchanged(grad_call(lat, g0, g1).reshape(8, 64, 1024), "z")
    dw = half_call(place, dw)
    total = parts[0]
    for part in parts[1:]:
        total = total + part.astype(F32)
    own, later = latent_call(place, fanned([total.astype(BF16)] * 4, "x"))
    later, outs = lax.optimization_barrier((later, outs))
    part = own + lax.ppermute(later, "z", behind).astype(F32)
    latent_grad = jnp.transpose(join_call(place, part, swapped(part)))
    attended = attended_call(place, fanned(outs, "y"))
    key_grad, value_grad = weight_call(place, fanned(dw, "y"))
    return attended, latent_grad, key_grad, value_grad


def solution(mesh):
    split = Mesh(mesh.devices.reshape(GROUPS, 4, 4, 2), ("z", "y", "x", "core"))
    seq, head = ("z", "y"), ("x", "core")
    in_specs = (P(seq, head), P(seq, None), P(seq), P(None, head), P(None, head), P(seq, head))
    out_specs = (P(seq, head), P(seq, None), P(seq, head), P(seq, head))
    return jax.shard_map(
        per_device, mesh=split, in_specs=in_specs, out_specs=out_specs, check_vma=False
    )
```

```python
import functools
import math

import jax
import jax.numpy as jnp
from jax import lax
from jax.experimental import pallas as pl
from jax.experimental.pallas import tpu as pltpu
from jax.sharding import Mesh
from jax.sharding import PartitionSpec as P

NOPE = 128
ROPE = 64
VDIM = 128
LATENT = 512
TOK = 128
SHARE = TOK // 8
ROWS = 4 * TOK
KEYS = 2 * ROWS
TILE = 256
SPAN = ROWS + TILE
PAY = 640
SCALE = 1.0 / math.sqrt(NOPE + ROPE)
LOG2E = math.log2(math.e)
HIDDEN = -1e30
GROUPS = 8
F32 = jnp.float32
BF16 = jnp.bfloat16
SMALL = pltpu.CompilerParams(vmem_limit_bytes=12 << 20)


def nt(a, b):
    return lax.dot_general(a, b, (((1,), (1,)), ((), ())), preferred_element_type=F32)


def nn(a, b):
    return lax.dot_general(a, b, (((1,), (0,)), ((), ())), preferred_element_type=F32)


def tn(a, b):
    return lax.dot_general(a, b, (((0,), (0,)), ((), ())), preferred_element_type=F32)


def in_hbm(x):
    return pltpu.with_memory_space_constraint(x, pltpu.HBM)


def pack_kernel(where_ref, q_ref, g_ref, *refs):
    piece_refs, sems = refs[:4], refs[4]
    y = where_ref[1]
    copies = []
    for k in range(4):
        to = (y + k) & 3
        for pair in range(2):
            left, at = pair * PAY, 4 * k + 2 * pair
            from_q = q_ref.at[:, pl.ds(pl.multiple_of(to * 768 + pair * 384, 128), 384)]
            from_g = g_ref.at[:, pl.ds(pl.multiple_of(to * 512 + pair * 256, 128), 256)]
            to_q = piece_refs[k].at[:, left : left + 384]
            to_g = piece_refs[k].at[:, left + 384 : left + PAY]
            copies.append(pltpu.make_async_copy(from_q, to_q, sems.at[at]))
            copies.append(pltpu.make_async_copy(from_g, to_g, sems.at[at + 1]))
    for copy in copies:
        copy.start()
    for copy in copies:
        copy.wait()


def pack_call(place, queries, out_grad):
    hbm = pl.BlockSpec(memory_space=pltpu.HBM)
    vmem = pl.BlockSpec(memory_space=pltpu.VMEM)
    return pl.pallas_call(
        pack_kernel,
        in_specs=[pl.BlockSpec(memory_space=pltpu.SMEM), hbm, hbm],
        out_specs=[vmem] * 4,
        out_shape=[jax.ShapeDtypeStruct((TOK, 2 * PAY), BF16)] * 4,
        scratch_shapes=[pltpu.SemaphoreType.DMA((16,))],
        cost_estimate=pl.CostEstimate(flops=0, bytes_accessed=2_600_000, transcendentals=0),
        compiler_params=SMALL,
        name="pack",
    )(place, in_hbm(queries), in_hbm(out_grad))


def pair_kernel(where_ref, *refs):
    pieces, mine_refs, other_refs, refs = refs[:4], refs[4:8], refs[8:12], refs[12:]
    wk_ref, wv_ref, refs = refs[0], refs[1], refs[2:]
    keep_ref, send_ref, out_refs, dw_ref = refs[0], refs[1], refs[2:6], refs[6]
    x_ref, l_ref, kcat, vals, bias, dk_acc, dv_acc, grads, attended, dl_acc = refs[7:]
    group, y, core, x = where_ref[0], where_ref[1], where_ref[2], where_ref[3]
    pair = pl.program_id(0)
    half = TOK // 2
    lane = lax.broadcasted_iota(jnp.int32, (KEYS, 128), 1)
    low = lane < ROPE
    for k in range(4):
        block = (y - k) & 3
        x_ref[pl.ds(pl.multiple_of(block * TOK, TOK), TOK), :] = pieces[k][...]

    @pl.when(pair == 0)
    def _():
        for j in range(4):
            for k in range(4):
                for own in range(2):
                    row = own * ROWS + ((y - k) & 3) * TOK + ((x - j) & 3) * SHARE
                    piece = slice((2 * k + own) * SHARE, (2 * k + own + 1) * SHARE)
                    at = pl.multiple_of(row + core * half, SHARE)
                    l_ref[pl.ds(at, SHARE), :] = mine_refs[j][piece]
                    at = pl.multiple_of(row + (1 - core) * half, SHARE)
                    l_ref[pl.ds(at, SHARE), :] = other_refs[j][piece]
        ids = l_ref[:, LATENT:].astype(F32)
        key_id = ids[:, ROPE : ROPE + 1]
        key_row = lax.broadcasted_iota(jnp.int32, (KEYS, 1), 0)
        key_id = jnp.where((key_row < ROWS) & (group == 0), -1.0, key_id)
        query_id = jnp.transpose(ids[ROWS:])[ROPE : ROPE + 1, :]
        for i in range(2):
            start = i * TILE
            at = lax.broadcasted_iota(jnp.int32, (SPAN, TILE), 0)
            by = lax.broadcasted_iota(jnp.int32, (SPAN, TILE), 1)
            seen = (key_id[start : start + SPAN] == query_id[:, start : start + TILE]) & (
                at <= by + ROWS
            )
            bias[i] = jnp.where(seen, 0.0, HIDDEN)

    lat = l_ref[:, :LATENT]
    tail = l_ref[:, LATENT:].astype(F32)
    keys_up = nn(lat, wk_ref[...])
    vals_up = nn(lat, wv_ref[...])
    vals[...] = vals_up.astype(BF16)
    rope_low = jnp.where(low, tail, 0.0)
    rope_high = pltpu.roll(rope_low, ROPE, 1)
    turned = pltpu.roll(keys_up[:, NOPE:], ROPE, 1)
    kcat[0, :, :NOPE] = keys_up[:, :NOPE].astype(BF16)
    kcat[0, :, NOPE:] = rope_low.astype(BF16)
    kcat[1, :, :NOPE] = jnp.where(low, 0.0, turned).astype(BF16)
    kcat[1, :, NOPE:] = jnp.where(low, turned, rope_high).astype(BF16)

    for h in range(2):
        v_turned = jnp.transpose(vals_up[:, h * VDIM : (h + 1) * VDIM]).astype(BF16)
        for i in range(2):
            start = i * TILE
            span = slice(start, start + SPAN)
            rows = slice(start, start + TILE)
            qc = x_ref[rows, h * NOPE : h * NOPE + 256]
            og = x_ref[rows, 384 + h * VDIM : 384 + (h + 1) * VDIM]
            s = nt(kcat[h, span, :], qc) * (SCALE * LOG2E) + bias[i]
            top = jnp.max(s, axis=0, keepdims=True)
            e = jnp.exp2(s - top)
            p = e * (1.0 / jnp.sum(e, axis=0, keepdims=True))
            pb = p.astype(BF16)
            out_t = nn(v_turned[:, span], pb).astype(BF16).astype(F32)
            attended[rows, h * VDIM : (h + 1) * VDIM] = jnp.transpose(out_t).astype(BF16)
            og_t = jnp.transpose(og.astype(F32))
            delta = jnp.sum(og_t * out_t, axis=0, keepdims=True)
            dp = nn(vals[span, h * VDIM : (h + 1) * VDIM], og_t.astype(BF16))
            ds = (p * (dp - delta) * SCALE).astype(BF16)
            dk = nn(ds, qc)
            dv = nn(pb, og)
            if i == 0:
                dk_acc[h, :SPAN, :] = dk
                dv_acc[:SPAN, :] = dv
            else:
                dk_acc[h, TILE : ROWS + TILE, :] += dk[:ROWS]
                dv_acc[TILE : ROWS + TILE, :] += dv[:ROWS]
                dk_acc[h, SPAN:, :] = dk[ROWS:]
                dv_acc[SPAN:, :] = dv[ROWS:]
        grads[:, 256 + h * VDIM : 256 + (h + 1) * VDIM] = dv_acc[...].astype(BF16)
    column = pl.ds(pl.multiple_of(pair * 256, 256), 256)
    for k in range(4):
        to = pl.multiple_of(((y + k) & 3) * TOK, TOK)
        out_refs[k][:, column] = attended[pl.ds(to, TOK), :]
    grads[:, :NOPE] = dk_acc[0, :, :NOPE].astype(BF16)
    mixed = jnp.where(low, dk_acc[1, :, NOPE:], dk_acc[1, :, :NOPE])
    grads[:, NOPE : 2 * NOPE] = pltpu.roll(mixed, ROPE, 1).astype(BF16)
    rope_grad = jnp.where(low, dk_acc[0, :, NOPE:], dk_acc[1, :, NOPE:])
    rope_grad = rope_grad + pltpu.roll(rope_grad, ROPE, 1)
    dl = nt(grads[:, :256], wk_ref[...]) + nt(grads[:, 256:], wv_ref[...])
    dw_ref[...] = tn(lat, grads[...]).astype(BF16)

    @pl.when(pair == 0)
    def _():
        dl_acc[:, :LATENT] = dl
        dl_acc[:, LATENT:] = rope_grad

    @pl.when(pair == 1)
    def _():
        dl_acc[:, :LATENT] += dl
        dl_acc[:, LATENT:] += rope_grad
        for k in range(4):
            for back in range(2):
                row = (1 - back) * ROWS + ((y + k) & 3) * TOK
                piece = slice(back * half, (back + 1) * half)
                at = pl.multiple_of(row + core * half, half)
                keep_ref[k, piece, :] = dl_acc[pl.ds(at, half), :].astype(BF16)
                at = pl.multiple_of(row + (1 - core) * half, half)
                send_ref[k, piece, :] = dl_acc[pl.ds(at, half), :].astype(BF16)


def pair_call(place, pieces, lats, key_weight, value_weight):
    def whole(*shape):
        return pl.BlockSpec(shape, lambda i, w: (0,) * len(shape))

    weight_spec = pl.BlockSpec((LATENT, 256), lambda i, w: (0, 2 * w[1] + i))
    x_spec = pl.BlockSpec((TOK, PAY), lambda i, w: (0, i))
    dw_spec = pl.BlockSpec((LATENT, 512), lambda i, w: (0, i))
    return pl.pallas_call(
        pair_kernel,
        grid_spec=pltpu.PrefetchScalarGridSpec(
            num_scalar_prefetch=1,
            grid=(2,),
            in_specs=[x_spec] * 4 + [whole(TOK, PAY)] * 8 + [weight_spec] * 2,
            out_specs=[whole(4, TOK, PAY)] * 2 + [whole(TOK, 512)] * 4 + [dw_spec],
            scratch_shapes=[
                pltpu.VMEM((ROWS, PAY), BF16),
                pltpu.VMEM((KEYS, PAY), BF16),
                pltpu.VMEM((2, KEYS, 256), BF16),
                pltpu.VMEM((KEYS, 256), BF16),
                pltpu.VMEM((2, SPAN, TILE), F32),
                pltpu.VMEM((2, KEYS, 256), F32),
                pltpu.VMEM((KEYS, VDIM), F32),
                pltpu.VMEM((KEYS, 512), BF16),
                pltpu.VMEM((ROWS, 256), BF16),
                pltpu.VMEM((KEYS, PAY), F32),
            ],
        ),
        out_shape=[pltpu.HBM((4, TOK, PAY), BF16)] * 2
        + [pltpu.HBM((TOK, 512), BF16)] * 4
        + [pltpu.HBM((LATENT, 1024), BF16)],
        compiler_params=pltpu.CompilerParams(vmem_limit_bytes=40 << 20),
        cost_estimate=pl.CostEstimate(
            flops=8_000_000_000, bytes_accessed=10_000_000, transcendentals=1_600_000
        ),
        name="pair",
    )(place, *pieces, *lats, in_hbm(key_weight), in_hbm(value_weight))


def latent_kernel(where_ref, *refs):
    terms, own_ref, later_ref, held = refs[:4], refs[4], refs[5], refs[6]
    x = where_ref[3]
    for k in range(4):
        held[(x - k) & 3] = terms[k][...].astype(F32)
    total = (held[0] + held[1]) + (held[2] + held[3])
    own_ref[...] = total[: TOK // 2]
    later_ref[...] = total[TOK // 2 :].astype(BF16)


def latent_call(place, terms):
    vmem = pl.BlockSpec(memory_space=pltpu.VMEM)
    return pl.pallas_call(
        latent_kernel,
        in_specs=[pl.BlockSpec(memory_space=pltpu.SMEM)] + [vmem] * 4,
        out_specs=[vmem] * 2,
        out_shape=[
            jax.ShapeDtypeStruct((TOK // 2, PAY), F32),
            jax.ShapeDtypeStruct((TOK // 2, PAY), BF16),
        ],
        scratch_shapes=[pltpu.VMEM((4, TOK, PAY), F32)],
        compiler_params=SMALL,
        name="latent",
    )(place, *terms)


def join_kernel(where_ref, mine_ref, other_ref, out_ref):
    first = where_ref[2] == 0
    mine, other = mine_ref[...], other_ref[...]
    rows = jnp.concatenate(
        [jnp.where(first, mine, other), jnp.where(first, other, mine)], axis=0
    )
    out_ref[...] = jnp.transpose(rows)[: LATENT + ROPE]


def join_call(place, mine, other):
    vmem = pl.BlockSpec(memory_space=pltpu.VMEM)
    return pl.pallas_call(
        join_kernel,
        in_specs=[pl.BlockSpec(memory_space=pltpu.SMEM), vmem, vmem],
        out_specs=vmem,
        out_shape=jax.ShapeDtypeStruct((LATENT + ROPE, TOK), F32),
        compiler_params=SMALL,
        name="join",
    )(place, mine, other)


def attended_kernel(where_ref, *refs):
    pieces, out_ref = refs[:4], refs[4]
    y = where_ref[1]
    for k in range(4):
        column = pl.multiple_of(((y - k) & 3) * 512, 512)
        out_ref[:, pl.ds(column, 512)] = pieces[k][...]


def attended_call(place, pieces):
    vmem = pl.BlockSpec(memory_space=pltpu.VMEM)
    return pl.pallas_call(
        attended_kernel,
        in_specs=[pl.BlockSpec(memory_space=pltpu.SMEM)] + [vmem] * 4,
        out_specs=vmem,
        out_shape=jax.ShapeDtypeStruct((TOK, 2048), BF16),
        compiler_params=SMALL,
        name="attended",
    )(place, *pieces)


def half_kernel(where_ref, sent_ref, *piece_refs):
    y = where_ref[1]
    for k in range(4):
        row = pl.ds(pl.multiple_of(((y + k) & 3) * 16, 16), 16)
        total = sent_ref[0, row, :].astype(F32)
        for z in range(1, GROUPS):
            total = total + sent_ref[z, row, :].astype(F32)
        piece_refs[k][...] = total.astype(BF16)


def half_call(place, sent):
    vmem = pl.BlockSpec(memory_space=pltpu.VMEM)
    return pl.pallas_call(
        half_kernel,
        in_specs=[pl.BlockSpec(memory_space=pltpu.SMEM), vmem],
        out_specs=[vmem] * 4,
        out_shape=[jax.ShapeDtypeStruct((16, 1024), BF16)] * 4,
        compiler_params=SMALL,
        name="half",
    )(place, sent)


def weight_kernel(where_ref, *refs):
    pieces, key_ref, value_ref = refs[:4], refs[4], refs[5]
    y = where_ref[1]
    for k in range(4):
        column = ((y - k) & 3) * 512
        for pair in range(2):
            here = pl.ds(pl.multiple_of(column + pair * 256, 256), 256)
            key_ref[:, here] = pieces[k][:, pair * 512 : pair * 512 + 256].astype(F32)
            value_ref[:, here] = pieces[k][:, pair * 512 + 256 : pair * 512 + 512].astype(F32)


def weight_call(place, pieces):
    vmem = pl.BlockSpec(memory_space=pltpu.VMEM)
    return pl.pallas_call(
        weight_kernel,
        in_specs=[pl.BlockSpec(memory_space=pltpu.SMEM)] + [vmem] * 4,
        out_specs=[vmem] * 2,
        out_shape=[jax.ShapeDtypeStruct((16, 2048), F32)] * 2,
        compiler_params=SMALL,
        name="weight",
    )(place, *pieces)


def exchanged(x, axes):
    return lax.all_to_all(x, axes, split_axis=0, concat_axis=0, tiled=True)


def moved(value, along, size, step):
    return lax.ppermute(value, along, [(i, (i + step) % size) for i in range(size)])


def fanned(pieces, along):
    return [p if k == 0 else moved(p, along, 4, k) for k, p in enumerate(pieces)]


def swapped(value):
    return lax.ppermute(value, "core", [(0, 1), (1, 0)])


def per_device(queries, latents, doc_ids, key_weight, value_weight, out_grad):
    core = lax.axis_index("core")
    place = [lax.axis_index("z"), lax.axis_index("y"), core, lax.axis_index("x")]
    place = jnp.stack(place).astype(jnp.int32)
    half = TOK // 2
    start = (core * 4 + lax.axis_index("x")) * SHARE
    rows = lax.dynamic_slice_in_dim(latents, start, SHARE)
    ids = lax.dynamic_slice_in_dim(doc_ids, start, SHARE)
    pay = jnp.concatenate(
        [rows, ids.astype(BF16)[:, None], jnp.zeros((SHARE, PAY - 577), BF16)], axis=1
    )
    ahead = [(i, i + 1) for i in range(GROUPS - 1)]
    behind = [(i + 1, i) for i in range(GROUPS - 1)]
    earlier = lax.ppermute(pay, "z", ahead)
    packed = pack_call(place, queries, out_grad)
    share = jnp.concatenate([earlier, pay], axis=0)
    share, packed = lax.optimization_barrier((share, packed))
    shares = fanned([share] * 4, "y")
    pieces = fanned(packed, "y")
    shares, pieces[1], pieces[3] = lax.optimization_barrier((shares, pieces[1], pieces[3]))
    mine = fanned([jnp.concatenate(shares, axis=0)] * 4, "x")
    lats = mine + [swapped(piece) for piece in mine]
    keep, send, *outs, dw = pair_call(place, pieces, lats, key_weight, value_weight)

    came = swapped(send)
    dw = half_call(place, exchanged(dw.reshape(8, 64, 1024), "z"))
    both = [keep[k].astype(F32) + came[k].astype(F32) for k in range(4)]
    parts = fanned([both[0]] + [part.astype(BF16) for part in both[1:]], "y")
    total = parts[0]
    for part in parts[1:]:
        total = total + part.astype(F32)
    total, outs = lax.optimization_barrier((total.astype(BF16), outs))
    terms, outs = lax.optimization_barrier((fanned([total] * 4, "x"), fanned(outs, "y")))
    own, later = latent_call(place, terms)
    later, dw = lax.optimization_barrier((lax.ppermute(later, "z", behind), fanned(dw, "y")))
    part = own + later.astype(F32)
    latent_grad = jnp.transpose(join_call(place, part, swapped(part)))
    attended = attended_call(place, outs)
    key_grad, value_grad = weight_call(place, dw)
    return attended, latent_grad, key_grad, value_grad


def solution(mesh):
    split = Mesh(mesh.devices.reshape(GROUPS, 4, 4, 2), ("z", "y", "x", "core"))
    seq, head = ("z", "y"), ("x", "core")
    in_specs = (P(seq, head), P(seq, None), P(seq), P(None, head), P(None, head), P(seq, head))
    out_specs = (P(seq, head), P(seq, None), P(seq, head), P(seq, head))
    return jax.shard_map(
        per_device, mesh=split, in_specs=in_specs, out_specs=out_specs, check_vma=False
    )
```

```python
import functools
import math

import jax
import jax.numpy as jnp
from jax import lax
from jax.experimental import pallas as pl
from jax.experimental.pallas import tpu as pltpu
from jax.sharding import Mesh
from jax.sharding import PartitionSpec as P

NOPE = 128
ROPE = 64
VDIM = 128
LATENT = 512
TOK = 128
SHARE = TOK // 8
ROWS = 4 * TOK
KEYS = 2 * ROWS
TILE = 256
SPAN = ROWS + TILE
PAY = 640
SCALE = 1.0 / math.sqrt(NOPE + ROPE)
LOG2E = math.log2(math.e)
HIDDEN = -1e30
GROUPS = 8
F32 = jnp.float32
BF16 = jnp.bfloat16
SMALL = pltpu.CompilerParams(vmem_limit_bytes=12 << 20)


def nt(a, b):
    return lax.dot_general(a, b, (((1,), (1,)), ((), ())), preferred_element_type=F32)


def nn(a, b):
    return lax.dot_general(a, b, (((1,), (0,)), ((), ())), preferred_element_type=F32)


def tn(a, b):
    return lax.dot_general(a, b, (((0,), (0,)), ((), ())), preferred_element_type=F32)


def in_hbm(x):
    return pltpu.with_memory_space_constraint(x, pltpu.HBM)


def pack_kernel(where_ref, q_ref, g_ref, *refs):
    piece_refs, sems = refs[:4], refs[4]
    y = where_ref[1]
    copies = []
    for k in range(4):
        to = (y + k) & 3
        for pair in range(2):
            left, at = pair * PAY, 4 * k + 2 * pair
            from_q = q_ref.at[:, pl.ds(pl.multiple_of(to * 768 + pair * 384, 128), 384)]
            from_g = g_ref.at[:, pl.ds(pl.multiple_of(to * 512 + pair * 256, 128), 256)]
            to_q = piece_refs[k].at[:, left : left + 384]
            to_g = piece_refs[k].at[:, left + 384 : left + PAY]
            copies.append(pltpu.make_async_copy(from_q, to_q, sems.at[at]))
            copies.append(pltpu.make_async_copy(from_g, to_g, sems.at[at + 1]))
    for copy in copies:
        copy.start()
    for copy in copies:
        copy.wait()


def pack_call(place, queries, out_grad):
    hbm = pl.BlockSpec(memory_space=pltpu.HBM)
    vmem = pl.BlockSpec(memory_space=pltpu.VMEM)
    return pl.pallas_call(
        pack_kernel,
        in_specs=[pl.BlockSpec(memory_space=pltpu.SMEM), hbm, hbm],
        out_specs=[vmem] * 4,
        out_shape=[jax.ShapeDtypeStruct((TOK, 2 * PAY), BF16)] * 4,
        scratch_shapes=[pltpu.SemaphoreType.DMA((16,))],
        cost_estimate=pl.CostEstimate(flops=0, bytes_accessed=2_600_000, transcendentals=0),
        compiler_params=SMALL,
        name="pack",
    )(place, in_hbm(queries), in_hbm(out_grad))


def pair_kernel(where_ref, *refs):
    pieces, mine_refs, other_refs, refs = refs[:4], refs[4:8], refs[8:12], refs[12:]
    wk_ref, wv_ref, refs = refs[0], refs[1], refs[2:]
    keep_ref, send_ref, out_refs, dw_ref = refs[0], refs[1], refs[2:6], refs[6]
    x_ref, l_ref, kcat, vals, bias, dk_acc, dv_acc, grads, attended, dl_acc = refs[7:]
    group, y, core, x = where_ref[0], where_ref[1], where_ref[2], where_ref[3]
    pair = pl.program_id(0)
    half = TOK // 2
    lane = lax.broadcasted_iota(jnp.int32, (KEYS, 128), 1)
    low = lane < ROPE
    for k in range(4):
        block = (y - k) & 3
        x_ref[pl.ds(pl.multiple_of(block * TOK, TOK), TOK), :] = pieces[k][...]

    @pl.when(pair == 0)
    def _():
        for j in range(4):
            for k in range(4):
                for own in range(2):
                    row = own * ROWS + ((y - k) & 3) * TOK + ((x - j) & 3) * SHARE
                    piece = slice((2 * k + own) * SHARE, (2 * k + own + 1) * SHARE)
                    at = pl.multiple_of(row + core * half, SHARE)
                    l_ref[pl.ds(at, SHARE), :] = mine_refs[j][piece]
                    at = pl.multiple_of(row + (1 - core) * half, SHARE)
                    l_ref[pl.ds(at, SHARE), :] = other_refs[j][piece]
        ids = l_ref[:, LATENT:].astype(F32)
        key_id = ids[:, ROPE : ROPE + 1]
        key_row = lax.broadcasted_iota(jnp.int32, (KEYS, 1), 0)
        key_id = jnp.where((key_row < ROWS) & (group == 0), -1.0, key_id)
        query_id = jnp.transpose(ids[ROWS:])[ROPE : ROPE + 1, :]
        for i in range(2):
            start = i * TILE
            at = lax.broadcasted_iota(jnp.int32, (SPAN, TILE), 0)
            by = lax.broadcasted_iota(jnp.int32, (SPAN, TILE), 1)
            seen = (key_id[start : start + SPAN] == query_id[:, start : start + TILE]) & (
                at <= by + ROWS
            )
            bias[i] = jnp.where(seen, 0.0, HIDDEN)

    lat = l_ref[:, :LATENT]
    tail = l_ref[:, LATENT:].astype(F32)
    keys_up = nn(lat, wk_ref[...])
    vals_up = nn(lat, wv_ref[...])
    vals[...] = vals_up.astype(BF16)
    rope_low = jnp.where(low, tail, 0.0)
    rope_high = pltpu.roll(rope_low, ROPE, 1)
    turned = pltpu.roll(keys_up[:, NOPE:], ROPE, 1)
    kcat[0, :, :NOPE] = keys_up[:, :NOPE].astype(BF16)
    kcat[0, :, NOPE:] = rope_low.astype(BF16)
    kcat[1, :, :NOPE] = jnp.where(low, 0.0, turned).astype(BF16)
    kcat[1, :, NOPE:] = jnp.where(low, turned, rope_high).astype(BF16)

    for h in range(2):
        v_turned = jnp.transpose(vals_up[:, h * VDIM : (h + 1) * VDIM]).astype(BF16)
        for i in range(2):
            start = i * TILE
            span = slice(start, start + SPAN)
            rows = slice(start, start + TILE)
            qc = x_ref[rows, h * NOPE : h * NOPE + 256]
            og = x_ref[rows, 384 + h * VDIM : 384 + (h + 1) * VDIM]
            s = nt(kcat[h, span, :], qc) * (SCALE * LOG2E) + bias[i]
            top = jnp.max(s, axis=0, keepdims=True)
            e = jnp.exp2(s - top)
            p = e * (1.0 / jnp.sum(e, axis=0, keepdims=True))
            pb = p.astype(BF16)
            out_t = nn(v_turned[:, span], pb).astype(BF16).astype(F32)
            attended[rows, h * VDIM : (h + 1) * VDIM] = jnp.transpose(out_t).astype(BF16)
            og_t = jnp.transpose(og.astype(F32))
            delta = jnp.sum(og_t * out_t, axis=0, keepdims=True)
            dp = nn(vals[span, h * VDIM : (h + 1) * VDIM], og_t.astype(BF16))
            ds = (p * (dp - delta) * SCALE).astype(BF16)
            dk = nn(ds, qc)
            dv = nn(pb, og)
            if i == 0:
                dk_acc[h, :SPAN, :] = dk
                dv_acc[:SPAN, :] = dv
            else:
                dk_acc[h, TILE : ROWS + TILE, :] += dk[:ROWS]
                dv_acc[TILE : ROWS + TILE, :] += dv[:ROWS]
                dk_acc[h, SPAN:, :] = dk[ROWS:]
                dv_acc[SPAN:, :] = dv[ROWS:]
        grads[:, 256 + h * VDIM : 256 + (h + 1) * VDIM] = dv_acc[...].astype(BF16)
    column = pl.ds(pl.multiple_of(pair * 256, 256), 256)
    for k in range(4):
        to = pl.multiple_of(((y + k) & 3) * TOK, TOK)
        out_refs[k][:, column] = attended[pl.ds(to, TOK), :]
    grads[:, :NOPE] = dk_acc[0, :, :NOPE].astype(BF16)
    mixed = jnp.where(low, dk_acc[1, :, NOPE:], dk_acc[1, :, :NOPE])
    grads[:, NOPE : 2 * NOPE] = pltpu.roll(mixed, ROPE, 1).astype(BF16)
    rope_grad = jnp.where(low, dk_acc[0, :, NOPE:], dk_acc[1, :, NOPE:])
    rope_grad = rope_grad + pltpu.roll(rope_grad, ROPE, 1)
    dl = nt(grads[:, :256], wk_ref[...]) + nt(grads[:, 256:], wv_ref[...])
    dw_ref[...] = tn(lat, grads[...]).astype(BF16)

    @pl.when(pair == 0)
    def _():
        dl_acc[:, :LATENT] = dl
        dl_acc[:, LATENT:] = rope_grad

    @pl.when(pair == 1)
    def _():
        dl_acc[:, :LATENT] += dl
        dl_acc[:, LATENT:] += rope_grad
        for k in range(4):
            for back in range(2):
                row = (1 - back) * ROWS + ((y + k) & 3) * TOK
                piece = slice(back * half, (back + 1) * half)
                at = pl.multiple_of(row + core * half, half)
                keep_ref[k, piece, :] = dl_acc[pl.ds(at, half), :].astype(BF16)
                at = pl.multiple_of(row + (1 - core) * half, half)
                send_ref[k, piece, :] = dl_acc[pl.ds(at, half), :].astype(BF16)


def pair_call(place, pieces, lats, key_weight, value_weight):
    def whole(*shape):
        return pl.BlockSpec(shape, lambda i, w: (0,) * len(shape))

    weight_spec = pl.BlockSpec((LATENT, 256), lambda i, w: (0, 2 * w[1] + i))
    x_spec = pl.BlockSpec((TOK, PAY), lambda i, w: (0, i))
    dw_spec = pl.BlockSpec((LATENT, 512), lambda i, w: (0, i))
    return pl.pallas_call(
        pair_kernel,
        grid_spec=pltpu.PrefetchScalarGridSpec(
            num_scalar_prefetch=1,
            grid=(2,),
            in_specs=[x_spec] * 4 + [whole(TOK, PAY)] * 8 + [weight_spec] * 2,
            out_specs=[whole(4, TOK, PAY)] * 2 + [whole(TOK, 512)] * 4 + [dw_spec],
            scratch_shapes=[
                pltpu.VMEM((ROWS, PAY), BF16),
                pltpu.VMEM((KEYS, PAY), BF16),
                pltpu.VMEM((2, KEYS, 256), BF16),
                pltpu.VMEM((KEYS, 256), BF16),
                pltpu.VMEM((2, SPAN, TILE), F32),
                pltpu.VMEM((2, KEYS, 256), F32),
                pltpu.VMEM((KEYS, VDIM), F32),
                pltpu.VMEM((KEYS, 512), BF16),
                pltpu.VMEM((ROWS, 256), BF16),
                pltpu.VMEM((KEYS, PAY), F32),
            ],
        ),
        out_shape=[pltpu.HBM((4, TOK, PAY), BF16)] * 2
        + [pltpu.HBM((TOK, 512), BF16)] * 4
        + [pltpu.HBM((LATENT, 1024), BF16)],
        compiler_params=pltpu.CompilerParams(vmem_limit_bytes=40 << 20),
        cost_estimate=pl.CostEstimate(
            flops=8_000_000_000, bytes_accessed=10_000_000, transcendentals=1_600_000
        ),
        name="pair",
    )(place, *pieces, *lats, in_hbm(key_weight), in_hbm(value_weight))


def latent_kernel(where_ref, *refs):
    terms, own_ref, later_ref, held = refs[:4], refs[4], refs[5], refs[6]
    x = where_ref[3]
    for k in range(4):
        held[(x - k) & 3] = terms[k][...].astype(F32)
    total = (held[0] + held[1]) + (held[2] + held[3])
    own_ref[...] = total[: TOK // 2]
    later_ref[...] = total[TOK // 2 :].astype(BF16)


def latent_call(place, terms):
    vmem = pl.BlockSpec(memory_space=pltpu.VMEM)
    return pl.pallas_call(
        latent_kernel,
        in_specs=[pl.BlockSpec(memory_space=pltpu.SMEM)] + [vmem] * 4,
        out_specs=[vmem] * 2,
        out_shape=[
            jax.ShapeDtypeStruct((TOK // 2, PAY), F32),
            jax.ShapeDtypeStruct((TOK // 2, PAY), BF16),
        ],
        scratch_shapes=[pltpu.VMEM((4, TOK, PAY), F32)],
        compiler_params=SMALL,
        name="latent",
    )(place, *terms)


def join_kernel(where_ref, mine_ref, other_ref, out_ref):
    first = where_ref[2] == 0
    mine, other = mine_ref[...], other_ref[...]
    rows = jnp.concatenate(
        [jnp.where(first, mine, other), jnp.where(first, other, mine)], axis=0
    )
    out_ref[...] = jnp.transpose(rows)[: LATENT + ROPE]


def join_call(place, mine, other):
    vmem = pl.BlockSpec(memory_space=pltpu.VMEM)
    return pl.pallas_call(
        join_kernel,
        in_specs=[pl.BlockSpec(memory_space=pltpu.SMEM), vmem, vmem],
        out_specs=vmem,
        out_shape=jax.ShapeDtypeStruct((LATENT + ROPE, TOK), F32),
        compiler_params=SMALL,
        name="join",
    )(place, mine, other)


def attended_kernel(where_ref, *refs):
    pieces, out_ref = refs[:4], refs[4]
    y = where_ref[1]
    for k in range(4):
        column = pl.multiple_of(((y - k) & 3) * 512, 512)
        out_ref[:, pl.ds(column, 512)] = pieces[k][...]


def attended_call(place, pieces):
    vmem = pl.BlockSpec(memory_space=pltpu.VMEM)
    return pl.pallas_call(
        attended_kernel,
        in_specs=[pl.BlockSpec(memory_space=pltpu.SMEM)] + [vmem] * 4,
        out_specs=vmem,
        out_shape=jax.ShapeDtypeStruct((TOK, 2048), BF16),
        compiler_params=SMALL,
        name="attended",
    )(place, *pieces)


def half_kernel(where_ref, sent_ref, *piece_refs):
    y = where_ref[1]
    for k in range(4):
        row = pl.ds(pl.multiple_of(((y + k) & 3) * 16, 16), 16)
        total = sent_ref[0, row, :].astype(F32)
        for z in range(1, GROUPS):
            total = total + sent_ref[z, row, :].astype(F32)
        piece_refs[k][...] = total.astype(BF16)


def half_call(place, sent):
    vmem = pl.BlockSpec(memory_space=pltpu.VMEM)
    return pl.pallas_call(
        half_kernel,
        in_specs=[pl.BlockSpec(memory_space=pltpu.SMEM), vmem],
        out_specs=[vmem] * 4,
        out_shape=[jax.ShapeDtypeStruct((16, 1024), BF16)] * 4,
        compiler_params=SMALL,
        name="half",
    )(place, sent)


def weight_kernel(where_ref, *refs):
    pieces, key_ref, value_ref = refs[:4], refs[4], refs[5]
    y = where_ref[1]
    for k in range(4):
        column = ((y - k) & 3) * 512
        for pair in range(2):
            here = pl.ds(pl.multiple_of(column + pair * 256, 256), 256)
            key_ref[:, here] = pieces[k][:, pair * 512 : pair * 512 + 256].astype(F32)
            value_ref[:, here] = pieces[k][:, pair * 512 + 256 : pair * 512 + 512].astype(F32)


def weight_call(place, pieces):
    vmem = pl.BlockSpec(memory_space=pltpu.VMEM)
    return pl.pallas_call(
        weight_kernel,
        in_specs=[pl.BlockSpec(memory_space=pltpu.SMEM)] + [vmem] * 4,
        out_specs=[vmem] * 2,
        out_shape=[jax.ShapeDtypeStruct((16, 2048), F32)] * 2,
        compiler_params=SMALL,
        name="weight",
    )(place, *pieces)


def exchanged(x, axes):
    return lax.all_to_all(x, axes, split_axis=0, concat_axis=0, tiled=True)


def moved(value, along, size, step):
    return lax.ppermute(value, along, [(i, (i + step) % size) for i in range(size)])


def fanned(pieces, along):
    return [p if k == 0 else moved(p, along, 4, k) for k, p in enumerate(pieces)]


def swapped(value):
    return lax.ppermute(value, "core", [(0, 1), (1, 0)])


def per_device(queries, latents, doc_ids, key_weight, value_weight, out_grad):
    core = lax.axis_index("core")
    place = [lax.axis_index("z"), lax.axis_index("y"), core, lax.axis_index("x")]
    place = jnp.stack(place).astype(jnp.int32)
    half = TOK // 2
    start = (core * 4 + lax.axis_index("x")) * SHARE
    rows = lax.dynamic_slice_in_dim(latents, start, SHARE)
    ids = lax.dynamic_slice_in_dim(doc_ids, start, SHARE)
    pay = jnp.concatenate(
        [rows, ids.astype(BF16)[:, None], jnp.zeros((SHARE, PAY - 577), BF16)], axis=1
    )
    ahead = [(i, i + 1) for i in range(GROUPS - 1)]
    behind = [(i + 1, i) for i in range(GROUPS - 1)]
    earlier = lax.ppermute(pay, "z", ahead)
    packed = pack_call(place, queries, out_grad)
    share = jnp.concatenate([earlier, pay], axis=0)
    share, packed = lax.optimization_barrier((share, packed))
    shares = fanned([share] * 4, "y")
    pieces = fanned(packed, "y")
    shares, pieces[1], pieces[3] = lax.optimization_barrier((shares, pieces[1], pieces[3]))
    mine = fanned([jnp.concatenate(shares, axis=0)] * 4, "x")
    lats = mine + [swapped(piece) for piece in mine]
    keep, send, *outs, dw = pair_call(place, pieces, lats, key_weight, value_weight)

    came = swapped(send)
    dw = half_call(place, exchanged(dw.reshape(8, 64, 1024), "z"))
    both = [keep[k].astype(F32) + came[k].astype(F32) for k in range(4)]
    parts = fanned([both[0]] + [part.astype(BF16) for part in both[1:]], "y")
    total = parts[0]
    for part in parts[1:]:
        total = total + part.astype(F32)
    total, outs = lax.optimization_barrier((total.astype(BF16), outs))
    terms, outs = lax.optimization_barrier((fanned([total] * 4, "x"), fanned(outs, "y")))
    own, later = latent_call(place, terms)
    attended = attended_call(place, outs)
    later, attended = lax.optimization_barrier((lax.ppermute(later, "z", behind), attended))
    dw = fanned(dw, "y")
    part = own + later.astype(F32)
    latent_grad = jnp.transpose(join_call(place, part, swapped(part)))
    key_grad, value_grad = weight_call(place, dw)
    return attended, latent_grad, key_grad, value_grad


def solution(mesh):
    split = Mesh(mesh.devices.reshape(GROUPS, 4, 4, 2), ("z", "y", "x", "core"))
    seq, head = ("z", "y"), ("x", "core")
    in_specs = (P(seq, head), P(seq, None), P(seq), P(None, head), P(None, head), P(seq, head))
    out_specs = (P(seq, head), P(seq, None), P(seq, head), P(seq, head))
    return jax.shard_map(
        per_device, mesh=split, in_specs=in_specs, out_specs=out_specs, check_vma=False
    )
```

```python
import functools
import math

import jax
import jax.numpy as jnp
from jax import lax
from jax.experimental import pallas as pl
from jax.experimental.pallas import tpu as pltpu
from jax.sharding import Mesh
from jax.sharding import PartitionSpec as P

NOPE = 128
ROPE = 64
VDIM = 128
LATENT = 512
TOK = 128
SHARE = TOK // 8
ROWS = 4 * TOK
KEYS = 2 * ROWS
TILE = 256
SPAN = ROWS + TILE
PAY = 640
SCALE = 1.0 / math.sqrt(NOPE + ROPE)
LOG2E = math.log2(math.e)
HIDDEN = -1e30
GROUPS = 8
F32 = jnp.float32
BF16 = jnp.bfloat16
SMALL = pltpu.CompilerParams(vmem_limit_bytes=12 << 20)


def nt(a, b):
    return lax.dot_general(a, b, (((1,), (1,)), ((), ())), preferred_element_type=F32)


def nn(a, b):
    return lax.dot_general(a, b, (((1,), (0,)), ((), ())), preferred_element_type=F32)


def tn(a, b):
    return lax.dot_general(a, b, (((0,), (0,)), ((), ())), preferred_element_type=F32)


def in_hbm(x):
    return pltpu.with_memory_space_constraint(x, pltpu.HBM)


def pack_kernel(where_ref, q_ref, g_ref, *refs):
    piece_refs, sems = refs[:4], refs[4]
    y = where_ref[1]
    copies = []
    for k in range(4):
        to = (y + k) & 3
        for pair in range(2):
            left, at = pair * PAY, 4 * k + 2 * pair
            from_q = q_ref.at[:, pl.ds(pl.multiple_of(to * 768 + pair * 384, 128), 384)]
            from_g = g_ref.at[:, pl.ds(pl.multiple_of(to * 512 + pair * 256, 128), 256)]
            to_q = piece_refs[k].at[:, left : left + 384]
            to_g = piece_refs[k].at[:, left + 384 : left + PAY]
            copies.append(pltpu.make_async_copy(from_q, to_q, sems.at[at]))
            copies.append(pltpu.make_async_copy(from_g, to_g, sems.at[at + 1]))
    for copy in copies:
        copy.start()
    for copy in copies:
        copy.wait()


def pack_call(place, queries, out_grad):
    hbm = pl.BlockSpec(memory_space=pltpu.HBM)
    vmem = pl.BlockSpec(memory_space=pltpu.VMEM)
    return pl.pallas_call(
        pack_kernel,
        in_specs=[pl.BlockSpec(memory_space=pltpu.SMEM), hbm, hbm],
        out_specs=[vmem] * 4,
        out_shape=[jax.ShapeDtypeStruct((TOK, 2 * PAY), BF16)] * 4,
        scratch_shapes=[pltpu.SemaphoreType.DMA((16,))],
        cost_estimate=pl.CostEstimate(flops=0, bytes_accessed=2_600_000, transcendentals=0),
        compiler_params=SMALL,
        name="pack",
    )(place, in_hbm(queries), in_hbm(out_grad))


def pair_kernel(where_ref, *refs):
    pieces, mine_refs, other_refs, refs = refs[:4], refs[4:8], refs[8:12], refs[12:]
    wk_ref, wv_ref, refs = refs[0], refs[1], refs[2:]
    keep_ref, send_ref, out_refs, dw_ref = refs[0], refs[1], refs[2:6], refs[6]
    x_ref, l_ref, kcat, vals, bias, dk_acc, dv_acc, grads, attended, dl_acc = refs[7:]
    group, y, core, x = where_ref[0], where_ref[1], where_ref[2], where_ref[3]
    pair = pl.program_id(0)
    half = TOK // 2
    lane = lax.broadcasted_iota(jnp.int32, (KEYS, 128), 1)
    low = lane < ROPE
    for k in range(4):
        block = (y - k) & 3
        x_ref[pl.ds(pl.multiple_of(block * TOK, TOK), TOK), :] = pieces[k][...]

    @pl.when(pair == 0)
    def _():
        for j in range(4):
            for k in range(4):
                for own in range(2):
                    row = own * ROWS + ((y - k) & 3) * TOK + ((x - j) & 3) * SHARE
                    piece = slice((2 * k + own) * SHARE, (2 * k + own + 1) * SHARE)
                    at = pl.multiple_of(row + core * half, SHARE)
                    l_ref[pl.ds(at, SHARE), :] = mine_refs[j][piece]
                    at = pl.multiple_of(row + (1 - core) * half, SHARE)
                    l_ref[pl.ds(at, SHARE), :] = other_refs[j][piece]
        ids = l_ref[:, LATENT:].astype(F32)
        key_id = ids[:, ROPE : ROPE + 1]
        key_row = lax.broadcasted_iota(jnp.int32, (KEYS, 1), 0)
        key_id = jnp.where((key_row < ROWS) & (group == 0), -1.0, key_id)
        query_id = jnp.transpose(ids[ROWS:])[ROPE : ROPE + 1, :]
        for i in range(2):
            start = i * TILE
            at = lax.broadcasted_iota(jnp.int32, (SPAN, TILE), 0)
            by = lax.broadcasted_iota(jnp.int32, (SPAN, TILE), 1)
            seen = (key_id[start : start + SPAN] == query_id[:, start : start + TILE]) & (
                at <= by + ROWS
            )
            bias[i] = jnp.where(seen, 0.0, HIDDEN)

    lat = l_ref[:, :LATENT]
    tail = l_ref[:, LATENT:].astype(F32)
    keys_up = nn(lat, wk_ref[...])
    vals_up = nn(lat, wv_ref[...])
    vals[...] = vals_up.astype(BF16)
    rope_low = jnp.where(low, tail, 0.0)
    rope_high = pltpu.roll(rope_low, ROPE, 1)
    turned = pltpu.roll(keys_up[:, NOPE:], ROPE, 1)
    kcat[0, :, :NOPE] = keys_up[:, :NOPE].astype(BF16)
    kcat[0, :, NOPE:] = rope_low.astype(BF16)
    kcat[1, :, :NOPE] = jnp.where(low, 0.0, turned).astype(BF16)
    kcat[1, :, NOPE:] = jnp.where(low, turned, rope_high).astype(BF16)

    for h in range(2):
        v_turned = jnp.transpose(vals_up[:, h * VDIM : (h + 1) * VDIM]).astype(BF16)
        for i in range(2):
            start = i * TILE
            span = slice(start, start + SPAN)
            rows = slice(start, start + TILE)
            qc = x_ref[rows, h * NOPE : h * NOPE + 256]
            og = x_ref[rows, 384 + h * VDIM : 384 + (h + 1) * VDIM]
            s = nt(kcat[h, span, :], qc) * (SCALE * LOG2E) + bias[i]
            top = jnp.max(s, axis=0, keepdims=True)
            e = jnp.exp2(s - top)
            p = e * (1.0 / jnp.sum(e, axis=0, keepdims=True))
            pb = p.astype(BF16)
            out_t = nn(v_turned[:, span], pb).astype(BF16).astype(F32)
            attended[rows, h * VDIM : (h + 1) * VDIM] = jnp.transpose(out_t).astype(BF16)
            og_t = jnp.transpose(og.astype(F32))
            delta = jnp.sum(og_t * out_t, axis=0, keepdims=True)
            dp = nn(vals[span, h * VDIM : (h + 1) * VDIM], og_t.astype(BF16))
            ds = (p * (dp - delta) * SCALE).astype(BF16)
            dk = nn(ds, qc)
            dv = nn(pb, og)
            if i == 0:
                dk_acc[h, :SPAN, :] = dk
                dv_acc[:SPAN, :] = dv
            else:
                dk_acc[h, TILE : ROWS + TILE, :] += dk[:ROWS]
                dv_acc[TILE : ROWS + TILE, :] += dv[:ROWS]
                dk_acc[h, SPAN:, :] = dk[ROWS:]
                dv_acc[SPAN:, :] = dv[ROWS:]
        grads[:, 256 + h * VDIM : 256 + (h + 1) * VDIM] = dv_acc[...].astype(BF16)
    column = pl.ds(pl.multiple_of(pair * 256, 256), 256)
    for k in range(4):
        to = pl.multiple_of(((y + k) & 3) * TOK, TOK)
        out_refs[k][:, column] = attended[pl.ds(to, TOK), :]
    grads[:, :NOPE] = dk_acc[0, :, :NOPE].astype(BF16)
    mixed = jnp.where(low, dk_acc[1, :, NOPE:], dk_acc[1, :, :NOPE])
    grads[:, NOPE : 2 * NOPE] = pltpu.roll(mixed, ROPE, 1).astype(BF16)
    rope_grad = jnp.where(low, dk_acc[0, :, NOPE:], dk_acc[1, :, NOPE:])
    rope_grad = rope_grad + pltpu.roll(rope_grad, ROPE, 1)
    dl = nt(grads[:, :256], wk_ref[...]) + nt(grads[:, 256:], wv_ref[...])
    dw_ref[...] = tn(lat, grads[...]).astype(BF16)

    @pl.when(pair == 0)
    def _():
        dl_acc[:, :LATENT] = dl
        dl_acc[:, LATENT:] = rope_grad

    @pl.when(pair == 1)
    def _():
        dl_acc[:, :LATENT] += dl
        dl_acc[:, LATENT:] += rope_grad
        for k in range(4):
            for back in range(2):
                row = (1 - back) * ROWS + ((y + k) & 3) * TOK
                piece = slice(back * half, (back + 1) * half)
                at = pl.multiple_of(row + core * half, half)
                keep_ref[k, piece, :] = dl_acc[pl.ds(at, half), :].astype(BF16)
                at = pl.multiple_of(row + (1 - core) * half, half)
                send_ref[k, piece, :] = dl_acc[pl.ds(at, half), :].astype(BF16)


def pair_call(place, pieces, lats, key_weight, value_weight):
    def whole(*shape):
        return pl.BlockSpec(shape, lambda i, w: (0,) * len(shape))

    weight_spec = pl.BlockSpec((LATENT, 256), lambda i, w: (0, 2 * w[1] + i))
    x_spec = pl.BlockSpec((TOK, PAY), lambda i, w: (0, i))
    dw_spec = pl.BlockSpec((LATENT, 512), lambda i, w: (0, i))
    return pl.pallas_call(
        pair_kernel,
        grid_spec=pltpu.PrefetchScalarGridSpec(
            num_scalar_prefetch=1,
            grid=(2,),
            in_specs=[x_spec] * 4 + [whole(TOK, PAY)] * 8 + [weight_spec] * 2,
            out_specs=[whole(4, TOK, PAY)] * 2 + [whole(TOK, 512)] * 4 + [dw_spec],
            scratch_shapes=[
                pltpu.VMEM((ROWS, PAY), BF16),
                pltpu.VMEM((KEYS, PAY), BF16),
                pltpu.VMEM((2, KEYS, 256), BF16),
                pltpu.VMEM((KEYS, 256), BF16),
                pltpu.VMEM((2, SPAN, TILE), F32),
                pltpu.VMEM((2, KEYS, 256), F32),
                pltpu.VMEM((KEYS, VDIM), F32),
                pltpu.VMEM((KEYS, 512), BF16),
                pltpu.VMEM((ROWS, 256), BF16),
                pltpu.VMEM((KEYS, PAY), F32),
            ],
        ),
        out_shape=[pltpu.HBM((4, TOK, PAY), BF16)] * 2
        + [pltpu.HBM((TOK, 512), BF16)] * 4
        + [pltpu.HBM((LATENT, 1024), BF16)],
        compiler_params=pltpu.CompilerParams(vmem_limit_bytes=40 << 20),
        cost_estimate=pl.CostEstimate(
            flops=8_000_000_000, bytes_accessed=10_000_000, transcendentals=1_600_000
        ),
        name="pair",
    )(place, *pieces, *lats, in_hbm(key_weight), in_hbm(value_weight))


def latent_kernel(where_ref, *refs):
    terms, own_ref, later_ref, held = refs[:4], refs[4], refs[5], refs[6]
    x = where_ref[3]
    for k in range(4):
        held[(x - k) & 3] = terms[k][...].astype(F32)
    total = (held[0] + held[1]) + (held[2] + held[3])
    own_ref[...] = total[: TOK // 2]
    later_ref[...] = total[TOK // 2 :].astype(BF16)


def latent_call(place, terms):
    vmem = pl.BlockSpec(memory_space=pltpu.VMEM)
    return pl.pallas_call(
        latent_kernel,
        in_specs=[pl.BlockSpec(memory_space=pltpu.SMEM)] + [vmem] * 4,
        out_specs=[vmem] * 2,
        out_shape=[
            jax.ShapeDtypeStruct((TOK // 2, PAY), F32),
            jax.ShapeDtypeStruct((TOK // 2, PAY), BF16),
        ],
        scratch_shapes=[pltpu.VMEM((4, TOK, PAY), F32)],
        compiler_params=SMALL,
        name="latent",
    )(place, *terms)


def join_kernel(where_ref, mine_ref, other_ref, out_ref):
    first = where_ref[2] == 0
    mine, other = mine_ref[...], other_ref[...]
    rows = jnp.concatenate(
        [jnp.where(first, mine, other), jnp.where(first, other, mine)], axis=0
    )
    out_ref[...] = jnp.transpose(rows)[: LATENT + ROPE]


def join_call(place, mine, other):
    vmem = pl.BlockSpec(memory_space=pltpu.VMEM)
    return pl.pallas_call(
        join_kernel,
        in_specs=[pl.BlockSpec(memory_space=pltpu.SMEM), vmem, vmem],
        out_specs=vmem,
        out_shape=jax.ShapeDtypeStruct((LATENT + ROPE, TOK), F32),
        compiler_params=SMALL,
        name="join",
    )(place, mine, other)


def attended_kernel(where_ref, *refs):
    pieces, out_ref = refs[:4], refs[4]
    y = where_ref[1]
    for k in range(4):
        column = pl.multiple_of(((y - k) & 3) * 512, 512)
        out_ref[:, pl.ds(column, 512)] = pieces[k][...]


def attended_call(place, pieces):
    vmem = pl.BlockSpec(memory_space=pltpu.VMEM)
    return pl.pallas_call(
        attended_kernel,
        in_specs=[pl.BlockSpec(memory_space=pltpu.SMEM)] + [vmem] * 4,
        out_specs=vmem,
        out_shape=jax.ShapeDtypeStruct((TOK, 2048), BF16),
        compiler_params=SMALL,
        name="attended",
    )(place, *pieces)


def half_kernel(where_ref, sent_ref, *piece_refs):
    y = where_ref[1]
    for k in range(4):
        row = pl.ds(pl.multiple_of(((y + k) & 3) * 16, 16), 16)
        total = sent_ref[0, row, :].astype(F32)
        for z in range(1, GROUPS):
            total = total + sent_ref[z, row, :].astype(F32)
        piece_refs[k][...] = total.astype(BF16)


def half_call(place, sent):
    vmem = pl.BlockSpec(memory_space=pltpu.VMEM)
    return pl.pallas_call(
        half_kernel,
        in_specs=[pl.BlockSpec(memory_space=pltpu.SMEM), vmem],
        out_specs=[vmem] * 4,
        out_shape=[jax.ShapeDtypeStruct((16, 1024), BF16)] * 4,
        compiler_params=SMALL,
        name="half",
    )(place, sent)


def weight_kernel(where_ref, *refs):
    pieces, key_ref, value_ref = refs[:4], refs[4], refs[5]
    y = where_ref[1]
    for k in range(4):
        column = ((y - k) & 3) * 512
        for pair in range(2):
            here = pl.ds(pl.multiple_of(column + pair * 256, 256), 256)
            key_ref[:, here] = pieces[k][:, pair * 512 : pair * 512 + 256].astype(F32)
            value_ref[:, here] = pieces[k][:, pair * 512 + 256 : pair * 512 + 512].astype(F32)


def weight_call(place, pieces):
    vmem = pl.BlockSpec(memory_space=pltpu.VMEM)
    return pl.pallas_call(
        weight_kernel,
        in_specs=[pl.BlockSpec(memory_space=pltpu.SMEM)] + [vmem] * 4,
        out_specs=[vmem] * 2,
        out_shape=[jax.ShapeDtypeStruct((16, 2048), F32)] * 2,
        compiler_params=SMALL,
        name="weight",
    )(place, *pieces)


def exchanged(x, axes):
    return lax.all_to_all(x, axes, split_axis=0, concat_axis=0, tiled=True)


def moved(value, along, size, step):
    return lax.ppermute(value, along, [(i, (i + step) % size) for i in range(size)])


def fanned(pieces, along):
    return [p if k == 0 else moved(p, along, 4, k) for k, p in enumerate(pieces)]


def swapped(value):
    return lax.ppermute(value, "core", [(0, 1), (1, 0)])


def per_device(queries, latents, doc_ids, key_weight, value_weight, out_grad):
    core = lax.axis_index("core")
    place = [lax.axis_index("z"), lax.axis_index("y"), core, lax.axis_index("x")]
    place = jnp.stack(place).astype(jnp.int32)
    half = TOK // 2
    start = (core * 4 + lax.axis_index("x")) * SHARE
    rows = lax.dynamic_slice_in_dim(latents, start, SHARE)
    ids = lax.dynamic_slice_in_dim(doc_ids, start, SHARE)
    pay = jnp.concatenate(
        [rows, ids.astype(BF16)[:, None], jnp.zeros((SHARE, PAY - 577), BF16)], axis=1
    )
    ahead = [(i, i + 1) for i in range(GROUPS - 1)]
    behind = [(i + 1, i) for i in range(GROUPS - 1)]
    earlier = lax.ppermute(pay, "z", ahead)
    packed = pack_call(place, queries, out_grad)
    share = jnp.concatenate([earlier, pay], axis=0)
    share, packed = lax.optimization_barrier((share, packed))
    shares = fanned([share] * 4, "y")
    pieces = fanned(packed, "y")
    shares, pieces[1], pieces[3] = lax.optimization_barrier((shares, pieces[1], pieces[3]))
    mine = fanned([jnp.concatenate(shares, axis=0)] * 4, "x")
    lats = mine + [swapped(piece) for piece in mine]
    keep, send, *outs, dw = pair_call(place, pieces, lats, key_weight, value_weight)

    came = swapped(send)
    dw = half_call(place, exchanged(dw.reshape(8, 64, 1024), "z"))
    both = [keep[k].astype(F32) + came[k].astype(F32) for k in range(4)]
    parts = fanned([both[0]] + [part.astype(BF16) for part in both[1:]], "y")
    total = parts[0]
    for part in parts[1:]:
        total = total + part.astype(F32)
    total = total.astype(BF16)
    terms, outs = lax.optimization_barrier((fanned([total] * 4, "x"), fanned(outs, "y")))
    own, later = latent_call(place, terms)
    attended = attended_call(place, outs)
    later, attended = lax.optimization_barrier((lax.ppermute(later, "z", behind), attended))
    dw = fanned(dw, "y")
    part = own + later.astype(F32)
    latent_grad = jnp.transpose(join_call(place, part, swapped(part)))
    key_grad, value_grad = weight_call(place, dw)
    return attended, latent_grad, key_grad, value_grad


def solution(mesh):
    split = Mesh(mesh.devices.reshape(GROUPS, 4, 4, 2), ("z", "y", "x", "core"))
    seq, head = ("z", "y"), ("x", "core")
    in_specs = (P(seq, head), P(seq, None), P(seq), P(None, head), P(None, head), P(seq, head))
    out_specs = (P(seq, head), P(seq, None), P(seq, head), P(seq, head))
    return jax.shard_map(
        per_device, mesh=split, in_specs=in_specs, out_specs=out_specs, check_vma=False
    )
```
